256 devices in a mesh: ctx: 64 (over z, x, core), heads: 4 (over y).
Axes of the slice: x: 4, y: 4, z: 8, core: 2. Of those that a mesh axis runs over, the one named last changes fastest.
Arguments:
- q_raw: bfloat16 [16384, 8192], P('ctx', 'heads'), may hold values from -60 to 60
- k_raw: bfloat16 [16384, 1024], P('ctx', 'heads'), may hold values from -60 to 60
- values: bfloat16 [16384, 1024], P('ctx', 'heads'), may hold values from -6 to 6
- saved_out: bfloat16 [16384, 8192], P('ctx', 'heads'), may hold values from -6 to 6
- out_grad: bfloat16 [16384, 8192], P('ctx', 'heads'), may hold values from -60 to 60
- q_gain: float32 [128], replicated, may hold values from 0.25 to 1.75
- k_gain: float32 [128], replicated, may hold values from 0.25 to 1.75
- ancestors: int32 [256, 32], P('ctx'), may hold values from -1 to 255, as said below
Outputs:
- dq_raw: bfloat16 [16384, 8192], P('ctx', 'heads')
- dk_raw: bfloat16 [16384, 1024], P('ctx', 'heads')
- dv: bfloat16 [16384, 1024], P('ctx', 'heads')
- q_gain_grad: float32 [128], replicated
- k_gain_grad: float32 [128], replicated
The draws below stay inside these ranges and needn't reach their ends.
Inputs may be any that keep to these rules, and one draw needn't show every extreme that they name: `ancestors`: the forest is 8 trees of 32 blocks each; in tree order, tree k holds blocks (k * 32 + 256 / 64 + b) mod 256 for b = 0 to 31. Row b lists, in tree order, every block on the path from its tree's first block to b, ending with b itself, then -1s. The first 16 blocks of a tree form its prompt, each the child of the block before it; every other block's parent is a block earlier in its tree, from the prompt's last block on.
All inputs are finite; a program needn't handle non-finite values.
Results may differ from the reference program's by a relative error of at most 0.0069.
Values may be sent and summed in bfloat16 or wider, within the bound.
A program may use at most 64 MiB of HBM per device.

```python
import math
import jax
import jax.numpy as jnp
from jax import lax

Q_HEADS = 64
KV_HEADS = 8
HEAD = 128
BLOCK = 64
TOK_DEV = 256
TOKENS = 16384
NBLK = 256
TREE_BLK = 32
PROMPT_BLK = 16


def draw_q_raw(key, part):
    key_scale, key_base = jax.random.split(key, 2)
    scales = jnp.exp(jax.random.uniform(key_scale, (TOKENS, Q_HEADS, 1), jnp.float32, 0.0, math.log(10.0)))
    entries = jnp.clip(jax.random.normal(key_base, (TOKENS, Q_HEADS, HEAD), jnp.float32), -5.0, 5.0)
    return (entries * scales).reshape(TOKENS, Q_HEADS * HEAD).astype(jnp.bfloat16)


def draw_k_raw(key, part):
    key_scale, key_base = jax.random.split(key, 2)
    scales = jnp.exp(jax.random.uniform(key_scale, (TOKENS, KV_HEADS, 1), jnp.float32, 0.0, math.log(10.0)))
    entries = jnp.clip(jax.random.normal(key_base, (TOKENS, KV_HEADS, HEAD), jnp.float32), -5.0, 5.0)
    return (entries * scales).reshape(TOKENS, KV_HEADS * HEAD).astype(jnp.bfloat16)


def draw_out_grad(key, part):
    key_scale, key_base = jax.random.split(key, 2)
    rising = math.log(3.0) / TOKENS * jnp.arange(TOKENS, dtype=jnp.float32)[:, None, None]
    scales = jnp.exp(rising + jax.random.uniform(key_scale, (TOKENS, Q_HEADS, 1), jnp.float32, 0.0, math.log(4.0)))
    entries = jnp.clip(jax.random.normal(key_base, (TOKENS, Q_HEADS, HEAD), jnp.float32), -5.0, 5.0)
    return (entries * scales).reshape(TOKENS, Q_HEADS * HEAD).astype(jnp.bfloat16)


def draw_ancestors(key, part):
    tree_count = NBLK // TREE_BLK
    shift_blocks = TOK_DEV // BLOCK
    within = jnp.arange(TREE_BLK, dtype=jnp.int32)

    def one_tree(tree_index):
        tree_key = jax.random.fold_in(key, tree_index)
        key_start, key_pick = jax.random.split(tree_key)
        starts = jax.random.randint(key_start, (TREE_BLK,), 0, 3) == 0
        spread = jnp.maximum(within - (PROMPT_BLK - 1), 1)
        picked = jax.random.randint(key_pick, (TREE_BLK,), 0, 1 << 20) % spread + (PROMPT_BLK - 1)
        parent = within - 1
        parent = jnp.where((within > PROMPT_BLK) & starts, picked, parent)

        def climb_up(level, loop_state):
            member, current = loop_state
            member = member | (current[:, None] == within[None, :])
            current = jnp.where(current >= 0, parent[jnp.maximum(current, 0)], -1)
            return (member, current)
        member, _ = lax.fori_loop(0, TREE_BLK, climb_up, (jnp.zeros((TREE_BLK, TREE_BLK), jnp.bool_), within))
        ordered = jnp.sort(jnp.where(member, within[None, :], TREE_BLK + within[None, :]), axis=1)
        return jnp.where(ordered < TREE_BLK, ordered + tree_index * TREE_BLK, -1)
    block_lists = jax.vmap(one_tree)(jnp.arange(tree_count, dtype=jnp.int32))
    block_lists = block_lists.reshape(NBLK, TREE_BLK).astype(jnp.int32)
    moved = jnp.where(block_lists >= 0, (block_lists + shift_blocks) % NBLK, -1)
    return jnp.roll(moved, shift_blocks, 0).astype(jnp.int32)


def block_scale(own_key, extent, pieces, smallest, largest):
    gain, own = 1.0, jax.random.fold_in(own_key, 6)
    for position, blocks in pieces:
        steps = jnp.exp(jax.random.uniform(jax.random.fold_in(own, position), (blocks,), jnp.float32, smallest / len(pieces), largest / len(pieces)))
        gain = gain * jnp.repeat(steps, extent[position] // blocks).reshape([-1 if axis == position else 1 for axis in range(len(extent))])
    return gain


def centred(rng, shape, scale, bound, cuts=(), held_as=jnp.bfloat16):
    values = scale * jax.random.normal(rng, shape, jnp.float32)
    if cuts:
        values = values * block_scale(rng, shape, cuts, -0.22, 0.18)
    return jnp.clip(values, -bound, bound).astype(held_as)


def setup_inputs(seed: int = 0) -> dict:
    seeds = jax.random.split(jax.random.key(seed), 9)
    return {
        "q_raw": draw_q_raw(jax.random.fold_in(seeds[8], 71), 0),
        "k_raw": draw_k_raw(jax.random.fold_in(seeds[8], 71), 0),
        "values": centred(seeds[2], (TOKENS, KV_HEADS * HEAD), 1.0, 6.0, ((0, 64), (1, 4))),
        "saved_out": centred(seeds[3], (TOKENS, Q_HEADS * HEAD), 1.0, 6.0, ((0, 64), (1, 4))),
        "out_grad": draw_out_grad(jax.random.fold_in(seeds[8], 71), 0),
        "q_gain": jnp.clip(1.0 + 0.15 * jax.random.normal(seeds[5], (HEAD,), jnp.float32), 0.25, 1.75),
        "k_gain": jnp.clip(1.0 + 0.15 * jax.random.normal(seeds[6], (HEAD,), jnp.float32), 0.25, 1.75),
        "ancestors": draw_ancestors(jax.random.fold_in(seeds[8], 71), 0),
    }


ROPE_BASE = 1000000.0
EPS = 1e-06

def rope_tables(positions, head_dim):
    half_dim = head_dim // 2
    frequency = jnp.exp(jnp.arange(half_dim, dtype=jnp.float32) * (-2.0 * math.log(ROPE_BASE) / head_dim))
    angles = positions.astype(jnp.float32)[:, None] * frequency[None, :]
    return (jnp.cos(angles), jnp.sin(angles))

def norm_rope(inputs, gain_vec, cos_table, sin_table):
    recip_rms = lax.rsqrt(lax.optimization_barrier(jnp.mean(inputs * inputs, -1, keepdims=True)) + EPS)
    scaled = inputs * recip_rms * gain_vec
    half_dim = inputs.shape[-1] // 2
    cos_part = cos_table[:, None, :]
    sin_part = sin_table[:, None, :]
    front_half = scaled[..., :half_dim]
    back_half = scaled[..., half_dim:]
    return jnp.concatenate([front_half * cos_part - back_half * sin_part, back_half * cos_part + front_half * sin_part], -1)

def norm_rope_back(inputs, gain_vec, cos_table, sin_table, upstream):
    half_dim = inputs.shape[-1] // 2
    cos_part = cos_table[:, None, :]
    sin_part = sin_table[:, None, :]
    front_half = upstream[..., :half_dim]
    back_half = upstream[..., half_dim:]
    unrotated = jnp.concatenate([front_half * cos_part + back_half * sin_part, back_half * cos_part - front_half * sin_part], -1)
    recip_rms = lax.rsqrt(lax.optimization_barrier(jnp.mean(inputs * inputs, -1, keepdims=True)) + EPS)
    normed = inputs * recip_rms
    gain_term = lax.optimization_barrier(jnp.sum(unrotated * normed, axis=(0, 1)))
    gain_grad = unrotated * gain_vec
    input_grad = recip_rms * (gain_grad - normed * lax.optimization_barrier(jnp.mean(gain_grad * normed, -1, keepdims=True)))
    return (input_grad, gain_term)

def reference(q_raw, k_raw, values, saved_out, out_grad, q_gain, k_gain, ancestors):
    inv_root = 1.0 / math.sqrt(HEAD)
    group_size = Q_HEADS // KV_HEADS
    shift_blocks = TOK_DEV // BLOCK
    q_raw = jnp.roll(q_raw, -TOK_DEV, 0)
    k_raw = jnp.roll(k_raw, -TOK_DEV, 0)
    values = jnp.roll(values, -TOK_DEV, 0)
    saved_out = jnp.roll(saved_out, -TOK_DEV, 0)
    out_grad = jnp.roll(out_grad, -TOK_DEV, 0)
    ancestors = jnp.roll(ancestors, -shift_blocks, 0)
    ancestors = jnp.where(ancestors >= 0, (ancestors - shift_blocks + NBLK) % NBLK, -1).astype(jnp.int32)
    offsets = jnp.arange(BLOCK, dtype=jnp.int32)
    depth_count = lax.optimization_barrier(jnp.sum((ancestors >= 0).astype(jnp.int32), 1))
    positions = (((depth_count - 1) * BLOCK)[:, None] + offsets[None, :]).reshape(TOKENS)
    cos_table, sin_table = rope_tables(positions, HEAD)
    q_float = q_raw.astype(jnp.float32).reshape(TOKENS, Q_HEADS, HEAD)
    k_float = k_raw.astype(jnp.float32).reshape(TOKENS, KV_HEADS, HEAD)
    q_rot = norm_rope(q_float, q_gain, cos_table, sin_table).astype(jnp.bfloat16)
    q_rot = q_rot.reshape(NBLK, BLOCK, KV_HEADS, group_size, HEAD)
    k_rot = norm_rope(k_float, k_gain, cos_table, sin_table).astype(jnp.bfloat16)
    v_heads = values.reshape(TOKENS, KV_HEADS, HEAD)
    grad_heads = out_grad.reshape(NBLK, BLOCK, KV_HEADS, group_size, HEAD)
    out_heads = saved_out.reshape(NBLK, BLOCK, KV_HEADS, group_size, HEAD)
    tree_len = TREE_BLK * BLOCK

    def per_block(loop_state, block_index):
        dk_acc, dv_acc = loop_state
        tree_first = block_index // TREE_BLK * TREE_BLK
        start_tok = (tree_first * BLOCK).astype(jnp.int32)
        tree_keys = lax.dynamic_slice_in_dim(k_rot, start_tok, tree_len, 0).astype(jnp.float32)
        tree_values = lax.dynamic_slice_in_dim(v_heads, start_tok, tree_len, 0).astype(jnp.float32)
        key_blocks = tree_first + jnp.arange(TREE_BLK, dtype=jnp.int32)
        block_vis = jnp.any(ancestors[block_index][:, None] == key_blocks[None, :], 0)
        key_tok = start_tok + jnp.arange(tree_len, dtype=jnp.int32)
        query_tok = block_index * BLOCK + offsets
        allowed = jnp.repeat(block_vis, BLOCK)[None, :] & (key_tok[None, :] <= query_tok[:, None])
        queries = q_rot[block_index].astype(jnp.float32)
        grad_rows = grad_heads[block_index].astype(jnp.float32)
        out_rows = out_heads[block_index].astype(jnp.float32)
        scores = jnp.einsum('ikgd,jkd->kgij', queries, tree_keys) * inv_root
        log_mass = jnp.log(lax.optimization_barrier(jnp.sum(jnp.where(allowed[None, None], jnp.exp(scores), 0.0), -1)))
        weights = jnp.where(allowed[None, None], jnp.exp(scores - log_mass[..., None]), 0.0)
        weights_low = lax.optimization_barrier(weights.astype(jnp.bfloat16)).astype(jnp.float32)
        row_delta = jnp.transpose(lax.optimization_barrier(jnp.sum(grad_rows * out_rows, -1)), (1, 2, 0))
        grad_prob = jnp.einsum('ikgd,jkd->kgij', grad_rows, tree_values)
        dscore = (weights * (grad_prob - row_delta[..., None]) * inv_root).astype(jnp.bfloat16)
        dscore = lax.optimization_barrier(dscore).astype(jnp.float32)
        dq_part = jnp.einsum('kgij,jkd->ikgd', dscore, tree_keys)
        dk_part = jnp.einsum('kgij,ikgd->jkd', dscore, queries)
        dv_part = jnp.einsum('kgij,ikgd->jkd', weights_low, grad_rows)
        current_k = lax.dynamic_slice_in_dim(dk_acc, start_tok, tree_len, 0)
        dk_acc = lax.dynamic_update_slice_in_dim(dk_acc, current_k + dk_part, start_tok, 0)
        current_v = lax.dynamic_slice_in_dim(dv_acc, start_tok, tree_len, 0)
        dv_acc = lax.dynamic_update_slice_in_dim(dv_acc, current_v + dv_part, start_tok, 0)
        return ((dk_acc, dv_acc), dq_part)
    zero_keys = jnp.zeros((TOKENS, KV_HEADS, HEAD), jnp.float32)
    (dk_rot, dv_acc), dq_parts = lax.scan(per_block, (zero_keys, zero_keys), jnp.arange(NBLK, dtype=jnp.int32))
    dq_rot = dq_parts.reshape(TOKENS, Q_HEADS, HEAD)
    dq_input, q_gain_grad = norm_rope_back(q_float, q_gain, cos_table, sin_table, dq_rot)
    dk_input, k_gain_grad = norm_rope_back(k_float, k_gain, cos_table, sin_table, dk_rot)
    dq_raw = jnp.roll(dq_input.astype(jnp.bfloat16).reshape(TOKENS, Q_HEADS * HEAD), TOK_DEV, 0)
    dk_raw = jnp.roll(dk_input.astype(jnp.bfloat16).reshape(TOKENS, KV_HEADS * HEAD), TOK_DEV, 0)
    dv = jnp.roll(dv_acc.astype(jnp.bfloat16).reshape(TOKENS, KV_HEADS * HEAD), TOK_DEV, 0)
    return (dq_raw, dk_raw, dv, q_gain_grad, k_gain_grad)
```

```python
import functools
import math

import jax
import jax.numpy as jnp
import numpy as np
from jax import lax
from jax.experimental import pallas as pl
from jax.experimental.pallas import tpu as pltpu
from jax.sharding import PartitionSpec as P

ROPE_BASE = 1000000.0
EPS = 1e-06
T = 256
D = 128
G = 8
BLK = 64
HALF = G * D
INV_ROOT = 1.0 / math.sqrt(D)
EXP_SCALE = INV_ROOT * math.log2(math.e)
F32 = jnp.float32
BF16 = jnp.bfloat16


def nn(a, b):
    return lax.dot_general(a, b, (((1,), (0,)), ((), ())), preferred_element_type=F32)


def nt(a, b):
    return lax.dot_general(a, b, (((1,), (1,)), ((), ())), preferred_element_type=F32)


def kernel(
    nz, q_hbm, k_ref, v_ref, so_hbm, do_hbm, qg_ref, kg_ref, anc_ref, fr_ref,
    dq_hbm, dk_ref, dv_ref, qgg_ref, kgg_ref,
    qx, dox, sox, kv, kvs, kt, aux, cosn, sinn, knorm, krec,
    qrt, qnt, qr, dot, dlt, dqt, esum, eb, gb, mask, eye, dkv, pbuf, red, dqo,
    qga, acc, ar1, ar2, ar3,
    lsem, xs, xr, kvs_sem, kvr_sem, ps_sem, pr_sem, os_sem, or_sem,
    s1, r1, s2, r2, s3, r3,
):
    c = lax.axis_index("ctx")
    y = lax.axis_index("heads")
    z = c // 8
    x = (c % 8) // 2
    h = c % 2
    nctx = nz * 8
    znext = (z + 1) % nz
    zprev = (z + nz - 1) % nz
    partner = c + 1 - 2 * h
    first = x == 0

    def rcopy(src, dst, ssem, rsem, ctx, heads=None):
        return pltpu.make_async_remote_copy(
            src_ref=src, dst_ref=dst, send_sem=ssem, recv_sem=rsem,
            device_id=(ctx, y if heads is None else heads),
            device_id_type=pl.DeviceIdType.MESH,
        )

    mine = pl.ds(pl.multiple_of(h * HALF, HALF), HALF)
    other = pl.ds(pl.multiple_of((1 - h) * HALF, HALF), HALF)
    loads = [
        pltpu.make_async_copy(src.at[:, mine], dst.at[h], lsem.at[n])
        for n, (src, dst) in enumerate(((q_hbm, qx), (do_hbm, dox), (so_hbm, sox)))
    ]
    for cp in loads:
        cp.start()

    bar = pltpu.get_barrier_semaphore()

    def greet(ctx, heads=None):
        pl.semaphore_signal(
            bar, inc=1, device_id=(ctx, y if heads is None else heads),
            device_id_type=pl.DeviceIdType.MESH,
        )

    for n in range(1, 8):
        greet(z * 8 + (c % 8 + n) % 8)
    for n in range(1, 4):
        greet(c, (y + n) % 4)
    for n in range(1, nz):
        greet((c + 8 * n) % nctx)
    for n in range(2):
        greet(znext * 8 + n)

    @pl.when(first)
    def _():
        for n in range(8):
            greet(zprev * 8 + n)

    anc = anc_ref[...]
    depth = jnp.sum((anc >= 0).astype(jnp.int32), axis=1, keepdims=True)
    off = lax.broadcasted_iota(jnp.int32, (BLK, D), 0)
    pos = jnp.concatenate(
        [(depth[b : b + 1] - 1) * BLK + off for b in range(4)], axis=0
    ).astype(F32)
    ang = pos * fr_ref[...]
    lane = lax.broadcasted_iota(jnp.int32, (T, D), 1)
    cos = jnp.cos(ang)
    sin = jnp.sin(ang)
    cosn[...] = cos
    sgn = jnp.where(lane < 64, -sin, sin)
    sinn[...] = sgn
    aux[h, 0:64, :] = cos.T[0:64]
    aux[h, 64:128, :] = sin.T[0:64]
    own_tree = jnp.where(first & (h == 0), zprev, z)
    ids = (lax.broadcasted_iota(jnp.int32, (32, 32), 0) + own_tree * 32 + 4) % (nz * 32)
    aux[h, 128:160, :] = jnp.concatenate(
        [
            jnp.broadcast_to(
                jnp.max(
                    jnp.where(jnp.broadcast_to(anc[b : b + 1], (32, 32)) == ids, 1.0, 0.0),
                    axis=1, keepdims=True,
                ),
                (32, BLK),
            )
            for b in range(4)
        ],
        axis=1,
    )
    eye[...] = jnp.where(
        lax.broadcasted_iota(jnp.int32, (T, T), 0) == lax.broadcasted_iota(jnp.int32, (T, T), 1),
        1.0, 0.0,
    ).astype(BF16)
    own_slot = jnp.where(first, 7 + h, 2 * x - 1 + h)
    other_slot = jnp.where(first, 8 - h, 2 * x - h)
    for hh in range(2):
        kf = k_ref[:, hh * D : (hh + 1) * D].astype(F32)
        rec = lax.rsqrt(jnp.mean(kf * kf, -1, keepdims=True) + EPS)
        normed = kf * rec
        scaled = normed * kg_ref[...]
        knorm[hh] = normed
        krec[hh] = jnp.broadcast_to(rec, (T, D))
        kvs[hh, 0] = (scaled * cos + pltpu.roll(scaled, 64, 1) * sgn).astype(BF16)
        kvs[hh, 1] = v_ref[:, hh * D : (hh + 1) * D]
    kv[own_slot] = kvs[h]
    dqt[...] = jnp.zeros_like(dqt)
    esum[...] = jnp.zeros_like(esum)
    qga[...] = jnp.zeros_like(qga)

    pl.semaphore_wait(bar, jnp.where(first, 8, 0) + (7 + 3 + nz - 1 + 2))

    kv_on_chip = rcopy(
        kvs.at[1 - h], kv.at[own_slot], kvs_sem.at[8], kvr_sem.at[own_slot], partner
    )
    xc = [
        rcopy(src.at[:, other], dst.at[h], xs.at[n], xr.at[n], partner)
        for n, (src, dst) in enumerate(((q_hbm, qx), (do_hbm, dox), (so_hbm, sox)))
    ]
    auxc = rcopy(aux.at[h], aux.at[h], xs.at[3], xr.at[3], partner)
    kv_on_chip.start()
    auxc.start()
    for cp in xc:
        cp.start()

    source = ~(first & (h == 0))
    position = jnp.where(first, 0, 2 * x - 1 + h)

    def kv_sends(act):
        for j in range(4):
            dest = znext * 8 if j == 0 else z * 8 + 2 * j
            ok = source & (True if j == 0 else j > x)

            @pl.when(ok)
            def _():
                for hh in range(2):
                    act(
                        rcopy(
                            kvs.at[hh], kv.at[position], kvs_sem.at[2 * j + hh],
                            kvr_sem.at[position], dest + hh,
                        )
                    )

    kv_sends(lambda cp: cp.start())

    gain = qg_ref[...]

    def prep(dev):
        tab_c = aux[dev, 0:64, :]
        tab_s = aux[dev, 64:128, :]
        ones = jnp.ones((8, D), BF16)

        def head(g, _):
            cols = pl.ds(pl.multiple_of(g * D, D), D)
            rows = pl.ds(pl.multiple_of(g * T, T), T)
            qt = nt(eye[0:D, 0:D], qx[dev, :, cols])
            rec = lax.rsqrt(jnp.mean(qt * qt, 0, keepdims=True) + EPS)
            normed = qt * rec
            qnt[dev, g] = normed
            qr[dev, g] = rec
            scaled = normed * gain
            a, b = scaled[0:64], scaled[64:128]
            qrt[dev, :, rows] = jnp.concatenate(
                [a * tab_c - b * tab_s, b * tab_c + a * tab_s], 0
            ).astype(BF16)
            grad = dox[dev, :, cols]
            dot[dev, :, rows] = nt(eye[0:D, 0:D], grad).astype(BF16)
            prod = grad.astype(F32) * sox[dev, :, cols].astype(F32)
            hi = prod.astype(BF16)
            lo = (prod - hi.astype(F32)).astype(BF16)
            dlt[dev, g] = (nt(ones, hi) + nt(ones, lo))[0:1]
            return 0

        lax.fori_loop(0, G, head, 0)

    def unit(order):
        early = order <= 1
        swapped = jnp.where(early, jnp.where(order == 0, 1 - h, h), order)
        slot = jnp.where(first, 8 - swapped, 2 * x - (swapped + 1) // 2)
        dev = jnp.where(first, jnp.where(swapped == 0, 1, 0), 1 - swapped % 2)
        return dev, slot, swapped

    def arrive(slot):
        rcopy(kvs.at[0], kv.at[slot], kvs_sem.at[0], kvr_sem.at[slot], c).wait_recv()

    def tiles(dev, slot, store, masked):
        def head(g, _):
            rows = pl.ds(pl.multiple_of(g * T, T), T)
            st = nn(kv[slot, 0], qrt[dev, :, rows])
            e = jnp.exp2(st * EXP_SCALE)
            if masked:
                e = e * mask[...]
            esum[dev, g] += jnp.sum(e, 0, keepdims=True)
            dp = nn(kv[slot, 1], dot[dev, :, rows])
            gg = (e * (dp - dlt[dev, g])).astype(BF16)
            eb[store, :, rows] = e.astype(BF16)
            gb[store, :, rows] = gg
            dqt[dev, g] += nn(kt[slot], gg)
            return 0

        lax.fori_loop(0, G, head, 0)

    def transpose_keys(slot):
        kt[slot] = nt(eye[0:D, 0:D], kv[slot, 0]).astype(BF16)

    def fill_mask(dev, index, causal):
        key = lax.broadcasted_iota(jnp.int32, (BLK, T), 0)
        tok = lax.broadcasted_iota(jnp.int32, (BLK, T), 1)
        for j in range(4):
            row = jnp.broadcast_to(aux[dev, pl.ds(128 + 4 * index + j, 1), :], (BLK, T))
            if causal:
                row = jnp.where(key + j * BLK <= tok, row, 0.0)
            mask[j * BLK : (j + 1) * BLK, :] = row

    def own_unit(order):
        dev, slot, store = unit(order)
        transpose_keys(slot)
        fill_mask(dev, jnp.where(slot == 8, 0, slot), True)
        tiles(dev, slot, store, True)

    for cp in loads:
        cp.wait()
    prep(h)
    own_unit(0)
    auxc.wait_recv()
    for cp in xc:
        cp.wait_recv()
    prep(1 - h)
    arrive(other_slot)
    own_unit(1)

    units = jnp.where(first, 9, 4 * x + 1)

    def later(order, _):
        dev, slot, store = unit(order)

        @pl.when(first | (order % 2 == 1))
        def _():
            arrive(slot)
            transpose_keys(slot)

        @pl.when(slot >= 4)
        def _():
            fill_mask(dev, slot, False)
            tiles(dev, slot, store, True)

        pl.when(slot < 4)(lambda: tiles(dev, slot, store, False))
        return 0

    lax.fori_loop(2, units, later, 0)

    def finish(dev):
        tab_c = aux[dev, 0:64, :]
        tab_s = aux[dev, 64:128, :]

        def head(g, _):
            cols = pl.ds(pl.multiple_of(g * D, D), D)
            rows = pl.ds(pl.multiple_of(g * T, T), T)
            inv = 1.0 / esum[dev, g]
            qrt[dev, :, rows] = (qrt[dev, :, rows].astype(F32) * (inv * INV_ROOT)).astype(BF16)
            dot[dev, :, rows] = (dot[dev, :, rows].astype(F32) * inv).astype(BF16)
            up = dqt[dev, g] * (inv * INV_ROOT)
            a, b = up[0:64], up[64:128]
            un = jnp.concatenate([a * tab_c + b * tab_s, b * tab_c - a * tab_s], 0)
            normed = qnt[dev, g]
            qga[...] += un * normed
            gg = un * gain
            dq = qr[dev, g] * (gg - normed * jnp.mean(gg * normed, 0, keepdims=True))
            dqo[dev, :, cols] = nt(eye[...], dq.astype(BF16)).astype(BF16)
            return 0

        lax.fori_loop(0, G, head, 0)

    finish(1 - h)
    dq_far = rcopy(dqo.at[1 - h], dq_hbm.at[:, mine], os_sem, or_sem, partner)
    dq_far.start()
    finish(h)
    dq_near = pltpu.make_async_copy(dqo.at[h], dq_hbm.at[:, mine], lsem.at[0])
    dq_near.start()

    slots = jnp.where(first, 9, 2 * x + 1)

    def partial_copy(slot):
        owner = jnp.where(
            first & (slot < 8), zprev * 8 + 1 + slot, z * 8 + 1 + jnp.where(slot == 8, 0, slot)
        ) % nctx
        place = jnp.where(first & (slot >= 7), 4, x)
        cp = rcopy(
            pbuf.at[slot], red.at[place, h], ps_sem.at[slot], pr_sem.at[place, h], owner
        )
        return owner, place, cp

    def second_pass(slot, _):
        dev = jnp.where(first & (slot < 8), 0, 1)
        store = jnp.where(first, 8 - slot, 2 * (2 * x - slot))
        dkv[0] = nt(gb[store], qrt[dev])
        dkv[1] = nt(eb[store], dot[dev])

        @pl.when(jnp.logical_not(first) & (slot < 2 * x))
        def _():
            dkv[0] += nt(gb[store - 1], qrt[0])
            dkv[1] += nt(eb[store - 1], dot[0])

        pbuf[slot] = dkv[...].astype(BF16)
        owner, place, cp = partial_copy(slot)

        @pl.when(slot == own_slot)
        def _():
            red[place, h] = pbuf[slot]

        pl.when(slot != own_slot)(lambda: cp.start())
        return 0

    lax.fori_loop(0, slots, second_pass, 0)

    own_place = jnp.where(first, 4, x)

    def take(place, head):
        rcopy(
            pbuf.at[0], red.at[place, head], ps_sem.at[0], pr_sem.at[place, head], c
        ).wait_recv()

    take(own_place, 1 - h)
    acc[...] = red[own_place].astype(F32)
    for j in (3, 2, 1, 0):

        @pl.when(source & (True if j == 0 else j > x))
        def _():
            for hh in range(2):
                take(j, hh)
                acc[hh] += red[j, hh].astype(F32)

    kga = jnp.zeros((1, D), F32)
    for hh in range(2):
        dk = acc[hh, 0]
        un = dk * cosn[...] - pltpu.roll(dk, 64, 1) * sinn[...]
        normed = knorm[hh]
        kga += jnp.sum(un * normed, 0, keepdims=True)
        gg = un * kg_ref[...]
        out = krec[hh] * (gg - normed * jnp.mean(gg * normed, -1, keepdims=True))
        dk_ref[:, hh * D : (hh + 1) * D] = out.astype(BF16)
        dv_ref[:, hh * D : (hh + 1) * D] = acc[hh, 1].astype(BF16)

    qcol = jnp.broadcast_to(jnp.sum(qga[...], 1, keepdims=True), (D, D)).T
    sub = lax.broadcasted_iota(jnp.int32, (8, D), 0)
    total = jnp.where(
        sub == 0, qcol[0:8], jnp.where(sub == 1, jnp.broadcast_to(kga, (8, D)), 0.0)
    )
    stages = (
        (ar1, s1, r1, 8, c % 8, lambda n: (z * 8 + (c % 8 + n) % 8, y)),
        (ar2, s2, r2, 4, y, lambda n: (c, (y + n) % 4)),
        (ar3, s3, r3, nz, z, lambda n: ((c + 8 * n) % nctx, y)),
    )
    for buf, ssem, rsem, count, me, peer in stages:
        buf[me] = total
        sends = []
        for n in range(1, count):
            ctx, heads = peer(n)
            sends.append(rcopy(buf.at[me], buf.at[me], ssem.at[n - 1], rsem.at[me], ctx, heads))
        for cp in sends:
            cp.start()
        for n in range(1, count):
            who = (me + n) % count
            rcopy(buf.at[who], buf.at[who], ssem.at[n - 1], rsem.at[who], c).wait_recv()
        total = jnp.sum(buf[...], 0)
        for cp in sends:
            cp.wait_send()
    qgg_ref[...] = total[0:1]
    kgg_ref[...] = total[1:2]

    kv_sends(lambda cp: cp.wait_send())
    kv_on_chip.wait_send()
    auxc.wait_send()
    for cp in xc:
        cp.wait_send()

    def drain(slot, _):
        pl.when(slot != own_slot)(lambda: partial_copy(slot)[2].wait_send())
        return 0

    lax.fori_loop(0, slots, drain, 0)
    dq_near.wait()
    dq_far.wait_send()
    dq_far.wait_recv()


def on_device(nz, q_raw, k_raw, values, saved_out, out_grad, q_gain, k_gain, ancestors):
    lanes = np.arange(D) % (D // 2)
    freq = jnp.asarray(
        np.exp(lanes * (-2.0 * math.log(ROPE_BASE) / D)).astype(np.float32)[None, :]
    )
    vm = pl.BlockSpec(memory_space=pltpu.VMEM)
    hbm = pl.BlockSpec(memory_space=pl.ANY)
    V = pltpu.VMEM
    dma = pltpu.SemaphoreType.DMA
    outs = pl.pallas_call(
        functools.partial(kernel, nz),
        out_shape=(
            jax.ShapeDtypeStruct(q_raw.shape, BF16),
            jax.ShapeDtypeStruct(k_raw.shape, BF16),
            jax.ShapeDtypeStruct(k_raw.shape, BF16),
            jax.ShapeDtypeStruct((1, D), F32),
            jax.ShapeDtypeStruct((1, D), F32),
        ),
        in_specs=[hbm, vm, vm, hbm, hbm, vm, vm, vm, vm],
        out_specs=(hbm, vm, vm, vm, vm),
        scratch_shapes=[
            V((2, T, HALF), BF16), V((2, T, HALF), BF16), V((2, T, HALF), BF16),
            V((9, 2, T, D), BF16), V((2, 2, T, D), BF16), V((9, D, T), BF16),
            V((2, 160, T), F32), V((T, D), F32), V((T, D), F32),
            V((2, T, D), F32), V((2, T, D), F32),
            V((2, D, G * T), BF16), V((2, G, D, T), F32), V((2, G, 1, T), F32),
            V((2, D, G * T), BF16), V((2, G, 1, T), F32), V((2, G, D, T), F32),
            V((2, G, 1, T), F32), V((13, T, G * T), BF16), V((13, T, G * T), BF16),
            V((T, T), F32), V((T, T), BF16), V((2, T, D), F32),
            V((9, 2, T, D), BF16), V((5, 2, 2, T, D), BF16), V((2, T, HALF), BF16),
            V((D, T), F32), V((2, 2, T, D), F32),
            V((8, 8, D), F32), V((4, 8, D), F32), V((nz, 8, D), F32),
            dma((3,)), dma((4,)), dma((4,)), dma((9,)), dma((9,)),
            dma((9,)), dma((5, 2)), dma, dma,
            dma((7,)), dma((8,)), dma((3,)), dma((4,)), dma((nz - 1,)), dma((nz,)),
        ],
        compiler_params=pltpu.CompilerParams(
            collective_id=0, has_side_effects=True, vmem_limit_bytes=63000000
        ),
    )(
        q_raw, k_raw, values, saved_out, out_grad,
        q_gain.reshape(D, 1), k_gain.reshape(1, D), ancestors, freq,
    )
    dq, dk, dv, qg, kg = outs
    return dq, dk, dv, qg.reshape(D), kg.reshape(D)


def solution(mesh):
    nz = mesh.shape["ctx"] // 8
    wide = P("ctx", "heads")
    return jax.shard_map(
        functools.partial(on_device, nz),
        mesh=mesh,
        in_specs=(wide, wide, wide, wide, wide, P(), P(), P("ctx", None)),
        out_specs=(wide, wide, wide, P(), P()),
        check_vma=False,
    )
```

```python
import functools
import math

import jax
import jax.numpy as jnp
import numpy as np
from jax import lax
from jax.experimental import pallas as pl
from jax.experimental.pallas import tpu as pltpu
from jax.sharding import PartitionSpec as P

ROPE_BASE = 1000000.0
EPS = 1e-06
T = 256
D = 128
G = 8
BLK = 64
HALF = G * D
UNROLL = 8
INV_ROOT = 1.0 / math.sqrt(D)
EXP_SCALE = INV_ROOT * math.log2(math.e)
F32 = jnp.float32
BF16 = jnp.bfloat16


def nn(a, b):
    return lax.dot_general(a, b, (((1,), (0,)), ((), ())), preferred_element_type=F32)


def nt(a, b):
    return lax.dot_general(a, b, (((1,), (1,)), ((), ())), preferred_element_type=F32)


def kernel(
    nz, q_hbm, k_ref, v_ref, so_hbm, do_hbm, qg_ref, kg_ref, anc_ref, fr_ref,
    dq_hbm, dk_ref, dv_ref, qgg_ref, kgg_ref,
    qx, dox, sox, kv, kvs, kt, aux, cosn, sinn, knorm, krec,
    qrt, qnt, qr, dot, dlt, dqt, esum, eb, gb, mask, eye, dkv, pbuf, rbuf, red, dqo,
    qga, acc, ar1, ar2, ar3,
    lsem, xs, xr, kvs_sem, kvr_sem, ps_sem, pr_sem, rr_sem, fs_sem, os_sem, or_sem,
    s1, r1, s2, r2, s3, r3,
):
    c = lax.axis_index("ctx")
    y = lax.axis_index("heads")
    z = c // 8
    x = (c % 8) // 2
    h = c % 2
    nctx = nz * 8
    znext = (z + 1) % nz
    zprev = (z + nz - 1) % nz
    partner = c + 1 - 2 * h
    first = x == 0

    def rcopy(src, dst, ssem, rsem, ctx, heads=None):
        return pltpu.make_async_remote_copy(
            src_ref=src, dst_ref=dst, send_sem=ssem, recv_sem=rsem,
            device_id=(ctx, y if heads is None else heads),
            device_id_type=pl.DeviceIdType.MESH,
        )

    mine = pl.ds(pl.multiple_of(h * HALF, HALF), HALF)
    other = pl.ds(pl.multiple_of((1 - h) * HALF, HALF), HALF)
    loads = [
        pltpu.make_async_copy(src.at[:, mine], dst.at[h], lsem.at[n])
        for n, (src, dst) in enumerate(((q_hbm, qx), (do_hbm, dox), (so_hbm, sox)))
    ]
    for cp in loads:
        cp.start()

    bar = pltpu.get_barrier_semaphore()

    def greet(ctx, heads=None):
        pl.semaphore_signal(
            bar, inc=1, device_id=(ctx, y if heads is None else heads),
            device_id_type=pl.DeviceIdType.MESH,
        )

    for n in range(1, 8):
        greet(z * 8 + (c % 8 + n) % 8)
    for n in range(1, 4):
        greet(c, (y + n) % 4)
    for n in range(1, nz):
        greet((c + 8 * n) % nctx)
    row = c % 8

    def greet_all(cond, base, places):
        @pl.when(cond)
        def _():
            for n in places:
                greet(base + n)

    greet_all(first, zprev * 8, range(1, 8))
    greet_all((row == 1) | (row >= 6), znext * 8, (0, 1))
    greet_all((row >= 2) & (row <= 5), znext * 8, (2, 3))
    greetings = (
        7 + 3 + nz - 1 + jnp.where(first, 3, 0) + jnp.where(x == 1, 4, 0) + jnp.where(row > 0, 2, 0)
    )

    anc = anc_ref[...]
    depth = jnp.sum((anc >= 0).astype(jnp.int32), axis=1, keepdims=True)
    off = lax.broadcasted_iota(jnp.int32, (BLK, D), 0)
    pos = jnp.concatenate(
        [(depth[b : b + 1] - 1) * BLK + off for b in range(4)], axis=0
    ).astype(F32)
    ang = pos * fr_ref[...]
    lane = lax.broadcasted_iota(jnp.int32, (T, D), 1)
    cos = jnp.cos(ang)
    sin = jnp.sin(ang)
    cosn[...] = cos
    sgn = jnp.where(lane < 64, -sin, sin)
    sinn[...] = sgn
    aux[h, 0:64, :] = cos.T[0:64]
    aux[h, 64:128, :] = sin.T[0:64]
    own_tree = jnp.where(first & (h == 0), zprev, z)
    ids = (lax.broadcasted_iota(jnp.int32, (32, 32), 0) + own_tree * 32 + 4) % (nz * 32)
    aux[h, 128:160, :] = jnp.concatenate(
        [
            jnp.broadcast_to(
                jnp.max(
                    jnp.where(jnp.broadcast_to(anc[b : b + 1], (32, 32)) == ids, 1.0, 0.0),
                    axis=1, keepdims=True,
                ),
                (32, BLK),
            )
            for b in range(4)
        ],
        axis=1,
    )
    eye[...] = jnp.where(
        lax.broadcasted_iota(jnp.int32, (T, T), 0) == lax.broadcasted_iota(jnp.int32, (T, T), 1),
        1.0, 0.0,
    ).astype(BF16)
    own_slot = jnp.where(first, 7 + h, 2 * x - 1 + h)
    other_slot = jnp.where(first, 8 - h, 2 * x - h)
    for hh in range(2):
        kf = k_ref[:, hh * D : (hh + 1) * D].astype(F32)
        rec = lax.rsqrt(jnp.mean(kf * kf, -1, keepdims=True) + EPS)
        normed = kf * rec
        scaled = normed * kg_ref[...]
        knorm[hh] = normed
        krec[hh] = jnp.broadcast_to(rec, (T, D))
        kvs[hh, 0] = (scaled * cos + pltpu.roll(scaled, 64, 1) * sgn).astype(BF16)
        kvs[hh, 1] = v_ref[:, hh * D : (hh + 1) * D]
    kv[own_slot] = kvs[h]
    dqt[...] = jnp.zeros_like(dqt)
    esum[...] = jnp.zeros_like(esum)
    qga[...] = jnp.zeros_like(qga)

    gain = jnp.broadcast_to(qg_ref[...], (D, D)).T[:, 0:1]

    def prep(dev):
        tab_c = aux[dev, 0:64, :]
        tab_s = aux[dev, 64:128, :]
        ones = jnp.ones((8, D), BF16)

        def head(g):
            cols = slice(g * D, (g + 1) * D)
            rows = slice(g * T, (g + 1) * T)
            qt = nt(eye[0:D, 0:D], qx[dev, :, cols])
            rec = lax.rsqrt(jnp.mean(qt * qt, 0, keepdims=True) + EPS)
            normed = qt * rec
            qnt[dev, g] = normed
            qr[dev, g] = rec
            scaled = normed * gain
            a, b = scaled[0:64], scaled[64:128]
            qrt[dev, :, rows] = jnp.concatenate(
                [a * tab_c - b * tab_s, b * tab_c + a * tab_s], 0
            ).astype(BF16)
            grad = dox[dev, :, cols]
            dot[dev, :, rows] = nt(eye[0:D, 0:D], grad).astype(BF16)
            prod = grad.astype(F32) * sox[dev, :, cols].astype(F32)
            hi = prod.astype(BF16)
            lo = (prod - hi.astype(F32)).astype(BF16)
            dlt[dev, g] = (nt(ones, hi) + nt(ones, lo))[0:1]

        for g in range(G):
            head(g)

    def unit(order):
        early = order <= 1
        swapped = jnp.where(early, jnp.where(order == 0, 1 - h, h), order)
        slot = jnp.where(first, 8 - swapped, 2 * x - (swapped + 1) // 2)
        dev = jnp.where(first, jnp.where(swapped == 0, 1, 0), 1 - swapped % 2)
        return dev, slot, swapped

    def arrive(slot):
        rcopy(kvs.at[0], kv.at[slot], kvs_sem.at[0], kvr_sem.at[slot], c).wait_recv()

    def tiles(dev, slot, store, masked):
        def heads(step, _):
            keys, vals, keys_t = kv[slot, 0], kv[slot, 1], kt[slot]
            low = []
            for u in range(UNROLL):
                g = step * UNROLL + u
                rows = pl.ds(pl.multiple_of(g * T, T), T)
                e = jnp.exp2(nn(keys, qrt[dev, :, rows]) * EXP_SCALE)
                if masked:
                    e = e * mask[...]
                dp = nn(vals, dot[dev, :, rows])
                gg = (e * (dp - dlt[dev, g])).astype(BF16)
                low.append((g, rows, e.astype(BF16), gg, jnp.sum(e, 0, keepdims=True)))
            for g, rows, el, gg, total in low:
                eb[store, :, rows] = el
                gb[store, :, rows] = gg
                esum[dev, g] += total
            for g, rows, el, gg, total in low:
                dqt[dev, g] += nn(keys_t, gg)
            return 0

        lax.fori_loop(0, G // UNROLL, heads, 0)

    def transpose_keys(slot):
        kt[slot] = nt(eye[0:D, 0:D], kv[slot, 0]).astype(BF16)

    def fill_mask(dev, index, causal):
        key = lax.broadcasted_iota(jnp.int32, (BLK, T), 0)
        tok = lax.broadcasted_iota(jnp.int32, (BLK, T), 1)
        for j in range(4):
            row = jnp.broadcast_to(aux[dev, pl.ds(128 + 4 * index + j, 1), :], (BLK, T))
            if causal:
                row = jnp.where(key + j * BLK <= tok, row, 0.0)
            mask[j * BLK : (j + 1) * BLK, :] = row

    def own_unit(order):
        dev, slot, store = unit(order)
        transpose_keys(slot)
        fill_mask(dev, jnp.where(slot == 8, 0, slot), True)
        tiles(dev, slot, store, True)

    for cp in loads:
        cp.wait()
    prep(h)
    own_unit(0)

    pl.semaphore_wait(bar, greetings)

    kv_on_chip = rcopy(
        kvs.at[1 - h], kv.at[own_slot], kvs_sem.at[8], kvr_sem.at[own_slot], partner
    )
    xc = [
        rcopy(src.at[:, other], dst.at[h], xs.at[n], xr.at[n], partner)
        for n, (src, dst) in enumerate(((q_hbm, qx), (do_hbm, dox), (so_hbm, sox)))
    ]
    auxc = rcopy(aux.at[h], aux.at[h], xs.at[3], xr.at[3], partner)
    kv_on_chip.start()
    auxc.start()
    for cp in xc:
        cp.start()

    source = ~(first & (h == 0))
    position = jnp.where(first, 0, 2 * x - 1 + h)

    def kv_sends(act):
        for j in range(4):
            dest = znext * 8 if j == 0 else z * 8 + 2 * j
            ok = source & (True if j == 0 else j > x)

            @pl.when(ok)
            def _():
                for hh in range(2):
                    act(
                        rcopy(
                            kvs.at[hh], kv.at[position], kvs_sem.at[2 * j + hh],
                            kvr_sem.at[position], dest + hh,
                        )
                    )

    kv_sends(lambda cp: cp.start())

    auxc.wait_recv()
    for cp in xc:
        cp.wait_recv()
    prep(1 - h)
    arrive(other_slot)
    own_unit(1)

    units = jnp.where(first, 9, 4 * x + 1)

    def later(order, _):
        dev, slot, store = unit(order)

        @pl.when(first | (order % 2 == 1))
        def _():
            arrive(slot)
            transpose_keys(slot)

        @pl.when(slot >= 4)
        def _():
            fill_mask(dev, slot, False)
            tiles(dev, slot, store, True)

        pl.when(slot < 4)(lambda: tiles(dev, slot, store, False))
        return 0

    lax.fori_loop(2, units, later, 0)

    def finish(dev):
        tab_c = aux[dev, 0:64, :]
        tab_s = aux[dev, 64:128, :]
        part = jnp.zeros((D, T), F32)
        for g in range(G):
            up = dqt[dev, g] * (esum[dev, g] * INV_ROOT)
            a, b = up[0:64], up[64:128]
            un = jnp.concatenate([a * tab_c + b * tab_s, b * tab_c - a * tab_s], 0)
            normed = qnt[dev, g]
            part += un * normed
            gg = un * gain
            dq = qr[dev, g] * (gg - normed * jnp.mean(gg * normed, 0, keepdims=True))
            dqo[dev, :, g * D : (g + 1) * D] = nt(eye[...], dq.astype(BF16)).astype(BF16)
        qga[...] += part

    def normalise(dev):
        for g in range(G):
            rows = slice(g * T, (g + 1) * T)
            inv = 1.0 / esum[dev, g]
            esum[dev, g] = inv
            qrt[dev, :, rows] = (qrt[dev, :, rows].astype(F32) * (inv * INV_ROOT)).astype(BF16)
            dot[dev, :, rows] = (dot[dev, :, rows].astype(F32) * inv).astype(BF16)

    for dev in range(2):
        normalise(dev)

    slots = jnp.where(first, 9, 2 * x + 1)

    def partial_copy(slot):
        owner = jnp.where(
            first & (slot < 8), zprev * 8 + 1 + slot, z * 8 + 1 + jnp.where(slot == 8, 0, slot)
        ) % nctx
        place = jnp.where(first & (slot >= 7), 4, x)
        cp = rcopy(
            pbuf.at[slot], red.at[place, h], ps_sem.at[slot], pr_sem.at[place, h], owner
        )
        return owner, place, cp

    def second_pass(slot, _):
        dev = jnp.where(first & (slot < 8), 0, 1)
        store = jnp.where(first, 8 - slot, 2 * (2 * x - slot))
        dkv[0] = nt(gb[store], qrt[dev])
        dkv[1] = nt(eb[store], dot[dev])

        @pl.when(jnp.logical_not(first) & (slot < 2 * x))
        def _():
            dkv[0] += nt(gb[store - 1], qrt[0])
            dkv[1] += nt(eb[store - 1], dot[0])

        pbuf[slot] = dkv[...].astype(BF16)
        owner, place, cp = partial_copy(slot)

        @pl.when(slot == own_slot)
        def _():
            red[place, h] = pbuf[slot]

        far = first & (slot >= 1) & (slot <= 4)
        pl.when((slot != own_slot) & jnp.logical_not(far))(lambda: cp.start())

        @pl.when(far)
        def _():
            place = jnp.clip(slot - 1, 0, 3)
            rcopy(
                pbuf.at[slot], rbuf.at[place], ps_sem.at[slot], rr_sem.at[place], z * 8 + 2 + h
            ).start()

        return 0

    lax.fori_loop(0, slots, second_pass, 0)

    finish(1 - h)
    dq_far = rcopy(dqo.at[1 - h], dq_hbm.at[:, mine], os_sem, or_sem, partner)
    dq_far.start()
    finish(h)
    dq_near = pltpu.make_async_copy(dqo.at[h], dq_hbm.at[:, mine], lsem.at[0])
    dq_near.start()

    def passing(n):
        return rcopy(
            rbuf.at[n], red.at[0, h], fs_sem.at[n], pr_sem.at[0, h], zprev * 8 + 2 + n
        )

    @pl.when(x == 1)
    def _():
        for n in range(4):
            rcopy(pbuf.at[0], rbuf.at[n], ps_sem.at[0], rr_sem.at[n], c).wait_recv()
            passing(n).start()

    own_place = jnp.where(first, 4, x)

    def take(place, head):
        rcopy(
            pbuf.at[0], red.at[place, head], ps_sem.at[0], pr_sem.at[place, head], c
        ).wait_recv()

    take(own_place, 1 - h)
    acc[...] = red[own_place].astype(F32)
    for j in (3, 2, 1, 0):

        @pl.when(source & (True if j == 0 else j > x))
        def _():
            for hh in range(2):
                take(j, hh)
                acc[hh] += red[j, hh].astype(F32)

    kga = jnp.zeros((1, D), F32)
    for hh in range(2):
        dk = acc[hh, 0]
        un = dk * cosn[...] - pltpu.roll(dk, 64, 1) * sinn[...]
        normed = knorm[hh]
        kga += jnp.sum(un * normed, 0, keepdims=True)
        gg = un * kg_ref[...]
        out = krec[hh] * (gg - normed * jnp.mean(gg * normed, -1, keepdims=True))
        dk_ref[:, hh * D : (hh + 1) * D] = out.astype(BF16)
        dv_ref[:, hh * D : (hh + 1) * D] = acc[hh, 1].astype(BF16)

    qcol = jnp.broadcast_to(jnp.sum(qga[...], 1, keepdims=True), (D, D)).T
    sub = lax.broadcasted_iota(jnp.int32, (8, D), 0)
    total = jnp.where(
        sub == 0, qcol[0:8], jnp.where(sub == 1, jnp.broadcast_to(kga, (8, D)), 0.0)
    )
    stages = (
        (ar1, s1, r1, 8, c % 8, lambda n: (z * 8 + (c % 8 + n) % 8, y)),
        (ar2, s2, r2, 4, y, lambda n: (c, (y + n) % 4)),
        (ar3, s3, r3, nz, z, lambda n: ((c + 8 * n) % nctx, y)),
    )
    for buf, ssem, rsem, count, me, peer in stages:
        buf[me] = total
        sends = []
        for n in range(1, count):
            ctx, heads = peer(n)
            sends.append(rcopy(buf.at[me], buf.at[me], ssem.at[n - 1], rsem.at[me], ctx, heads))
        for cp in sends:
            cp.start()
        for n in range(1, count):
            who = (me + n) % count
            rcopy(buf.at[who], buf.at[who], ssem.at[n - 1], rsem.at[who], c).wait_recv()
        total = jnp.sum(buf[...], 0)
        for cp in sends:
            cp.wait_send()
    qgg_ref[...] = total[0:1]
    kgg_ref[...] = total[1:2]

    kv_sends(lambda cp: cp.wait_send())
    kv_on_chip.wait_send()
    auxc.wait_send()
    for cp in xc:
        cp.wait_send()

    def drain(slot, _):
        pl.when(slot != own_slot)(lambda: partial_copy(slot)[2].wait_send())
        return 0

    lax.fori_loop(0, slots, drain, 0)

    @pl.when(x == 1)
    def _():
        for n in range(4):
            passing(n).wait_send()

    dq_near.wait()
    dq_far.wait_send()
    dq_far.wait_recv()


def emit(dq, dk, dv, qg, kg, dq_out, dk_out, dv_out, qg_out, kg_out, big, small, isem, osem):
    pieces = [(dk, small.at[0], dk_out), (dv, small.at[1], dv_out)]
    for n in range(4):
        rows = pl.ds(n * 64, 64)
        pieces.append((dq.at[rows], big.at[rows], dq_out.at[rows]))
    ins = [pltpu.make_async_copy(a, b, isem.at[n]) for n, (a, b, _) in enumerate(pieces)]
    outs = [pltpu.make_async_copy(b, o, osem.at[n]) for n, (_, b, o) in enumerate(pieces)]
    for cp in ins:
        cp.start()
    qg_out[...] = qg[0]
    kg_out[...] = kg[0]
    for a, b in zip(ins, outs):
        a.wait()
        b.start()
    for b in outs:
        b.wait()


def on_device(nz, q_raw, k_raw, values, saved_out, out_grad, q_gain, k_gain, ancestors):
    lanes = np.arange(D) % (D // 2)
    freq = jnp.asarray(
        np.exp(lanes * (-2.0 * math.log(ROPE_BASE) / D)).astype(np.float32)[None, :]
    )
    vm = pl.BlockSpec(memory_space=pltpu.VMEM)
    hbm = pl.BlockSpec(memory_space=pl.ANY)
    V = pltpu.VMEM
    dma = pltpu.SemaphoreType.DMA
    outs = pl.pallas_call(
        functools.partial(kernel, nz),
        out_shape=(
            jax.ShapeDtypeStruct(q_raw.shape, BF16),
            jax.ShapeDtypeStruct(k_raw.shape, BF16),
            jax.ShapeDtypeStruct(k_raw.shape, BF16),
            jax.ShapeDtypeStruct((1, D), F32),
            jax.ShapeDtypeStruct((1, D), F32),
        ),
        in_specs=[hbm, vm, vm, hbm, hbm, vm, vm, vm, vm],
        out_specs=(hbm, vm, vm, vm, vm),
        scratch_shapes=[
            V((2, T, HALF), BF16), V((2, T, HALF), BF16), V((2, T, HALF), BF16),
            V((9, 2, T, D), BF16), V((2, 2, T, D), BF16), V((9, D, T), BF16),
            V((2, 160, T), F32), V((T, D), F32), V((T, D), F32),
            V((2, T, D), F32), V((2, T, D), F32),
            V((2, D, G * T), BF16), V((2, G, D, T), F32), V((2, G, 1, T), F32),
            V((2, D, G * T), BF16), V((2, G, 1, T), F32), V((2, G, D, T), F32),
            V((2, G, 1, T), F32), V((13, T, G * T), BF16), V((13, T, G * T), BF16),
            V((T, T), F32), V((T, T), BF16), V((2, T, D), F32),
            V((9, 2, T, D), BF16), V((4, 2, T, D), BF16), V((5, 2, 2, T, D), BF16), V((2, T, HALF), BF16),
            V((D, T), F32), V((2, 2, T, D), F32),
            V((8, 8, D), F32), V((4, 8, D), F32), V((nz, 8, D), F32),
            dma((3,)), dma((4,)), dma((4,)), dma((9,)), dma((9,)),
            dma((9,)), dma((5, 2)), dma((4,)), dma((4,)), dma, dma,
            dma((7,)), dma((8,)), dma((3,)), dma((4,)), dma((nz - 1,)), dma((nz,)),
        ],
        compiler_params=pltpu.CompilerParams(
            collective_id=0, has_side_effects=True, vmem_limit_bytes=63000000
        ),
    )(
        q_raw, k_raw, values, saved_out, out_grad,
        q_gain.reshape(1, D), k_gain.reshape(1, D), ancestors, freq,
    )
    return pl.pallas_call(
        emit,
        out_shape=(
            jax.ShapeDtypeStruct(q_raw.shape, BF16),
            jax.ShapeDtypeStruct(k_raw.shape, BF16),
            jax.ShapeDtypeStruct(k_raw.shape, BF16),
            jax.ShapeDtypeStruct((D,), F32),
            jax.ShapeDtypeStruct((D,), F32),
        ),
        in_specs=[hbm, hbm, hbm, vm, vm],
        out_specs=(hbm, hbm, hbm, vm, vm),
        scratch_shapes=[
            V(q_raw.shape, BF16), V((2,) + k_raw.shape, BF16), dma((6,)), dma((6,)),
        ],
    )(*outs)


def solution(mesh):
    nz = mesh.shape["ctx"] // 8
    wide = P("ctx", "heads")
    return jax.shard_map(
        functools.partial(on_device, nz),
        mesh=mesh,
        in_specs=(wide, wide, wide, wide, wide, P(), P(), P("ctx", None)),
        out_specs=(wide, wide, wide, P(), P()),
        check_vma=False,
    )
```

```python
import functools
import math

import jax
import jax.numpy as jnp
import numpy as np
from jax import lax
from jax.experimental import pallas as pl
from jax.experimental.pallas import tpu as pltpu
from jax.sharding import PartitionSpec as P

ROPE_BASE = 1000000.0
EPS = 1e-06
T = 256
D = 128
G = 8
BLK = 64
HALF = G * D
UNROLL = 8
INV_ROOT = 1.0 / math.sqrt(D)
EXP_SCALE = INV_ROOT * math.log2(math.e)
F32 = jnp.float32
BF16 = jnp.bfloat16


def nn(a, b):
    return lax.dot_general(a, b, (((1,), (0,)), ((), ())), preferred_element_type=F32)


def nt(a, b):
    return lax.dot_general(a, b, (((1,), (1,)), ((), ())), preferred_element_type=F32)


def kernel(
    nz, q_hbm, k_ref, v_ref, so_hbm, do_hbm, qg_ref, kg_ref, anc_ref, fr_ref,
    dq_hbm, dk_ref, dv_ref, qgg_ref, kgg_ref,
    qx, dox, sox, kv, kvs, kt, aux, cosn, sinn, knorm, krec,
    qrt, qnt, qr, dot, dlt, dqt, esum, eb, gb, mask, eye, dkv, pbuf, rbuf, red, dqo,
    qga, kga, toff, tblk, acc, ar1, ar2, ar3,
    lsem, xs, xr, kvs_sem, kvr_sem, ps_sem, pr_sem, rr_sem, fs_sem, os_sem, or_sem,
    s1, r1, s2, r2, s3, r3,
):
    c = lax.axis_index("ctx")
    y = lax.axis_index("heads")
    z = c // 8
    x = (c % 8) // 2
    h = c % 2
    nctx = nz * 8
    znext = (z + 1) % nz
    zprev = (z + nz - 1) % nz
    partner = c + 1 - 2 * h
    first = x == 0

    def rcopy(src, dst, ssem, rsem, ctx, heads=None):
        return pltpu.make_async_remote_copy(
            src_ref=src, dst_ref=dst, send_sem=ssem, recv_sem=rsem,
            device_id=(ctx, y if heads is None else heads),
            device_id_type=pl.DeviceIdType.MESH,
        )

    mine = pl.ds(pl.multiple_of(h * HALF, HALF), HALF)
    other = pl.ds(pl.multiple_of((1 - h) * HALF, HALF), HALF)
    loads = [
        pltpu.make_async_copy(src.at[:, mine], dst.at[h], lsem.at[n])
        for n, (src, dst) in enumerate(((q_hbm, qx), (do_hbm, dox), (so_hbm, sox)))
    ]
    for cp in loads:
        cp.start()

    bar = pltpu.get_barrier_semaphore()

    def greet(ctx, heads=None):
        pl.semaphore_signal(
            bar, inc=1, device_id=(ctx, y if heads is None else heads),
            device_id_type=pl.DeviceIdType.MESH,
        )

    for n in range(1, 8):
        greet(z * 8 + (c % 8 + n) % 8)
    for n in range(1, 4):
        greet(c, (y + n) % 4)
    for n in range(1, nz):
        greet((c + 8 * n) % nctx)
    row = c % 8

    def greet_all(cond, base, places):
        @pl.when(cond)
        def _():
            for n in places:
                greet(base + n)

    greet_all(first, zprev * 8, range(1, 8))
    greet_all((row == 1) | (row >= 6), znext * 8, (0, 1))
    greet_all((row >= 2) & (row <= 5), znext * 8, (2, 3))
    greetings = (
        7 + 3 + nz - 1 + jnp.where(first, 3, 0) + jnp.where(x == 1, 4, 0) + jnp.where(row > 0, 2, 0)
    )

    anc = anc_ref[...]
    depth = jnp.sum((anc >= 0).astype(jnp.int32), axis=1, keepdims=True)
    off = lax.broadcasted_iota(jnp.int32, (BLK, D), 0)
    pos = jnp.concatenate(
        [(depth[b : b + 1] - 1) * BLK + off for b in range(4)], axis=0
    ).astype(F32)
    ang = pos * fr_ref[...]
    lane = lax.broadcasted_iota(jnp.int32, (T, D), 1)
    cos = jnp.cos(ang)
    sin = jnp.sin(ang)
    cosn[...] = cos
    sgn = jnp.where(lane < 64, -sin, sin)
    sinn[...] = sgn
    aux[h, 0:64, :] = cos.T[0:64]
    aux[h, 64:128, :] = sin.T[0:64]
    own_tree = jnp.where(first & (h == 0), zprev, z)
    ids = (lax.broadcasted_iota(jnp.int32, (32, 32), 0) + own_tree * 32 + 4) % (nz * 32)
    aux[h, 128:160, :] = jnp.concatenate(
        [
            jnp.broadcast_to(
                jnp.max(
                    jnp.where(jnp.broadcast_to(anc[b : b + 1], (32, 32)) == ids, 1.0, 0.0),
                    axis=1, keepdims=True,
                ),
                (32, BLK),
            )
            for b in range(4)
        ],
        axis=1,
    )
    eye[...] = jnp.where(
        lax.broadcasted_iota(jnp.int32, (T, T), 0) == lax.broadcasted_iota(jnp.int32, (T, T), 1),
        1.0, 0.0,
    ).astype(BF16)
    own_slot = jnp.where(first, 7 + h, 2 * x - 1 + h)
    other_slot = jnp.where(first, 8 - h, 2 * x - h)
    for hh in range(2):
        kf = k_ref[:, hh * D : (hh + 1) * D].astype(F32)
        rec = lax.rsqrt(jnp.mean(kf * kf, -1, keepdims=True) + EPS)
        normed = kf * rec
        scaled = normed * kg_ref[...]
        knorm[hh] = normed
        krec[hh] = jnp.broadcast_to(rec, (T, D))
        kvs[hh, 0] = (scaled * cos + pltpu.roll(scaled, 64, 1) * sgn).astype(BF16)
        kvs[hh, 1] = v_ref[:, hh * D : (hh + 1) * D]
    kv[own_slot] = kvs[h]
    dqt[...] = jnp.zeros_like(dqt)
    esum[...] = jnp.zeros_like(esum)
    qga[...] = jnp.zeros_like(qga)
    kga[...] = jnp.zeros_like(kga)
    sign = jnp.where(lane[0:1] < 64, -1.0, 1.0)
    ang_off = off.astype(F32) * fr_ref[...]
    toff[0] = jnp.cos(ang_off)
    toff[1] = jnp.sin(ang_off) * sign

    gain = jnp.broadcast_to(qg_ref[...], (D, D)).T[:, 0:1]

    def prep(dev):
        tab_c = aux[dev, 0:64, :]
        tab_s = aux[dev, 64:128, :]
        ones = jnp.ones((8, D), BF16)

        def head(g):
            cols = slice(g * D, (g + 1) * D)
            rows = slice(g * T, (g + 1) * T)
            qt = nt(eye[0:D, 0:D], qx[dev, :, cols])
            rec = lax.rsqrt(jnp.mean(qt * qt, 0, keepdims=True) + EPS)
            normed = qt * rec
            qnt[dev, g] = normed
            qr[dev, g] = rec
            scaled = normed * gain
            a, b = scaled[0:64], scaled[64:128]
            qrt[dev, :, rows] = jnp.concatenate(
                [a * tab_c - b * tab_s, b * tab_c + a * tab_s], 0
            ).astype(BF16)
            grad = dox[dev, :, cols]
            dot[dev, :, rows] = nt(eye[0:D, 0:D], grad).astype(BF16)
            prod = grad.astype(F32) * sox[dev, :, cols].astype(F32)
            hi = prod.astype(BF16)
            lo = (prod - hi.astype(F32)).astype(BF16)
            dlt[dev, g] = (nt(ones, hi) + nt(ones, lo))[0:1]

        for g in range(G):
            head(g)

    def unit(order):
        early = order <= 1
        swapped = jnp.where(early, jnp.where(order == 0, 1 - h, h), order)
        slot = jnp.where(first, 8 - swapped, 2 * x - (swapped + 1) // 2)
        dev = jnp.where(first, jnp.where(swapped == 0, 1, 0), 1 - swapped % 2)
        return dev, slot, swapped

    def arrive(slot):
        rcopy(kvs.at[0], kv.at[slot], kvs_sem.at[0], kvr_sem.at[slot], c).wait_recv()

    def tiles(dev, slot, store, masked):
        def heads(step, _):
            keys, vals, keys_t = kv[slot, 0], kv[slot, 1], kt[slot]
            low = []
            for u in range(UNROLL):
                g = step * UNROLL + u
                rows = pl.ds(pl.multiple_of(g * T, T), T)
                e = jnp.exp2(nn(keys, qrt[dev, :, rows]) * EXP_SCALE)
                if masked:
                    e = e * mask[...]
                dp = nn(vals, dot[dev, :, rows])
                gg = (e * (dp - dlt[dev, g])).astype(BF16)
                low.append((g, rows, e.astype(BF16), gg, jnp.sum(e, 0, keepdims=True)))
            for g, rows, el, gg, total in low:
                eb[store, :, rows] = el
                gb[store, :, rows] = gg
                esum[dev, g] += total
            for g, rows, el, gg, total in low:
                dqt[dev, g] += nn(keys_t, gg)
            return 0

        lax.fori_loop(0, G // UNROLL, heads, 0)

    def transpose_keys(slot):
        kt[slot] = nt(eye[0:D, 0:D], kv[slot, 0]).astype(BF16)

    def fill_mask(dev, index, causal):
        key = lax.broadcasted_iota(jnp.int32, (BLK, T), 0)
        tok = lax.broadcasted_iota(jnp.int32, (BLK, T), 1)
        for j in range(4):
            row = jnp.broadcast_to(aux[dev, pl.ds(128 + 4 * index + j, 1), :], (BLK, T))
            if causal:
                row = jnp.where(key + j * BLK <= tok, row, 0.0)
            mask[j * BLK : (j + 1) * BLK, :] = row

    def own_unit(order):
        dev, slot, store = unit(order)
        transpose_keys(slot)
        fill_mask(dev, jnp.where(slot == 8, 0, slot), True)
        tiles(dev, slot, store, True)

    for cp in loads:
        cp.wait()
    prep(h)
    own_unit(0)

    pl.semaphore_wait(bar, greetings)

    kv_on_chip = rcopy(
        kvs.at[1 - h], kv.at[own_slot], kvs_sem.at[8], kvr_sem.at[own_slot], partner
    )
    xc = [
        rcopy(src.at[:, other], dst.at[h], xs.at[n], xr.at[n], partner)
        for n, (src, dst) in enumerate(((q_hbm, qx), (do_hbm, dox), (so_hbm, sox)))
    ]
    auxc = rcopy(aux.at[h], aux.at[h], xs.at[3], xr.at[3], partner)
    kv_on_chip.start()
    auxc.start()
    for cp in xc:
        cp.start()

    source = ~(first & (h == 0))
    position = jnp.where(first, 0, 2 * x - 1 + h)

    def kv_sends(act):
        for j in range(4):
            dest = znext * 8 if j == 0 else z * 8 + 2 * j
            ok = source & (True if j == 0 else j > x)

            @pl.when(ok)
            def _():
                for hh in range(2):
                    act(
                        rcopy(
                            kvs.at[hh], kv.at[position], kvs_sem.at[2 * j + hh],
                            kvr_sem.at[position], dest + hh,
                        )
                    )

    kv_sends(lambda cp: cp.start())

    auxc.wait_recv()
    for cp in xc:
        cp.wait_recv()
    prep(1 - h)
    arrive(other_slot)
    own_unit(1)

    tri = jnp.where(
        lax.broadcasted_iota(jnp.int32, (32, 32), 0) >= lax.broadcasted_iota(jnp.int32, (32, 32), 1),
        1.0, 0.0,
    ).astype(BF16)
    count = jnp.ones((32, 1), F32)
    for dev in range(2):
        seen = aux[dev, 128:160, :]
        upto = nn(tri, seen.astype(BF16))
        count = jnp.maximum(count, jnp.max(seen * upto, axis=1, keepdims=True))
    ang_blk = jnp.broadcast_to((count - 1.0) * BLK, (32, D)) * fr_ref[...]
    tblk[0] = jnp.cos(ang_blk)
    tblk[1] = jnp.sin(ang_blk) * sign

    units = jnp.where(first, 9, 4 * x + 1)

    def later(order, _):
        dev, slot, store = unit(order)

        @pl.when(first | (order % 2 == 1))
        def _():
            arrive(slot)
            transpose_keys(slot)

        @pl.when(slot >= 4)
        def _():
            fill_mask(dev, slot, False)
            tiles(dev, slot, store, True)

        pl.when(slot < 4)(lambda: tiles(dev, slot, store, False))
        return 0

    lax.fori_loop(2, units, later, 0)

    def finish(dev):
        tab_c = aux[dev, 0:64, :]
        tab_s = aux[dev, 64:128, :]
        part = jnp.zeros((D, T), F32)
        for g in range(G):
            up = dqt[dev, g] * (esum[dev, g] * INV_ROOT)
            a, b = up[0:64], up[64:128]
            un = jnp.concatenate([a * tab_c + b * tab_s, b * tab_c - a * tab_s], 0)
            normed = qnt[dev, g]
            part += un * normed
            gg = un * gain
            dq = qr[dev, g] * (gg - normed * jnp.mean(gg * normed, 0, keepdims=True))
            dqo[dev, :, g * D : (g + 1) * D] = nt(eye[...], dq.astype(BF16)).astype(BF16)
        qga[...] += part

    def normalise(dev):
        for g in range(G):
            rows = slice(g * T, (g + 1) * T)
            inv = 1.0 / esum[dev, g]
            esum[dev, g] = inv
            qrt[dev, :, rows] = (qrt[dev, :, rows].astype(F32) * (inv * INV_ROOT)).astype(BF16)
            dot[dev, :, rows] = (dot[dev, :, rows].astype(F32) * inv).astype(BF16)

    for dev in range(2):
        normalise(dev)

    slots = jnp.where(first, 9, 2 * x + 1)

    def partial_copy(slot):
        owner = jnp.where(
            first & (slot < 8), zprev * 8 + 1 + slot, z * 8 + 1 + jnp.where(slot == 8, 0, slot)
        ) % nctx
        place = jnp.where(first & (slot >= 7), 4, x)
        cp = rcopy(
            pbuf.at[slot], red.at[place, h], ps_sem.at[slot], pr_sem.at[place, h], owner
        )
        return owner, place, cp

    def second_pass(slot, _):
        dev = jnp.where(first & (slot < 8), 0, 1)
        store = jnp.where(first, 8 - slot, 2 * (2 * x - slot))
        dkv[0] = nt(gb[store], qrt[dev])
        dkv[1] = nt(eb[store], dot[dev])

        @pl.when(jnp.logical_not(first) & (slot < 2 * x))
        def _():
            dkv[0] += nt(gb[store - 1], qrt[0])
            dkv[1] += nt(eb[store - 1], dot[0])

        pbuf[slot] = dkv[...].astype(BF16)
        gains = jnp.zeros((1, D), F32)
        for j in range(4):
            place = pl.ds(4 * jnp.where(slot == 8, 0, slot) + j, 1)
            part = slice(j * BLK, (j + 1) * BLK)
            cos_b, sin_b = tblk[0, place, :], tblk[1, place, :]
            cos_k = cos_b * toff[0] - sin_b * toff[1]
            sin_k = sin_b * toff[0] + cos_b * toff[1]
            dkp = dkv[0, part]
            key = kv[slot, 0, part].astype(F32)
            gains += jnp.sum(
                (dkp * cos_k - pltpu.roll(dkp, 64, 1) * sin_k)
                * (key * cos_k - pltpu.roll(key, 64, 1) * sin_k),
                0, keepdims=True,
            )
        kga[...] += gains
        owner, place, cp = partial_copy(slot)

        @pl.when(slot == own_slot)
        def _():
            red[place, h] = pbuf[slot]

        far = first & (slot >= 1) & (slot <= 4)
        pl.when((slot != own_slot) & jnp.logical_not(far))(lambda: cp.start())

        @pl.when(far)
        def _():
            place = jnp.clip(slot - 1, 0, 3)
            rcopy(
                pbuf.at[slot], rbuf.at[place], ps_sem.at[slot], rr_sem.at[place], z * 8 + 2 + h
            ).start()

        return 0

    lax.fori_loop(0, slots, second_pass, 0)

    finish(1 - h)
    dq_far = rcopy(dqo.at[1 - h], dq_hbm.at[:, mine], os_sem, or_sem, partner)
    dq_far.start()
    finish(h)
    dq_near = pltpu.make_async_copy(dqo.at[h], dq_hbm.at[:, mine], lsem.at[0])
    dq_near.start()

    qcol = jnp.broadcast_to(jnp.sum(qga[...], 1, keepdims=True), (D, D)).T
    sub = lax.broadcasted_iota(jnp.int32, (8, D), 0)
    ksum = jnp.broadcast_to(kga[...] / kg_ref[...], (8, D))
    total = jnp.where(sub == 0, qcol[0:8], jnp.where(sub == 1, ksum, 0.0))
    stages = (
        (ar1, s1, r1, 8, c % 8, lambda n: (z * 8 + (c % 8 + n) % 8, y)),
        (ar2, s2, r2, 4, y, lambda n: (c, (y + n) % 4)),
        (ar3, s3, r3, nz, z, lambda n: ((c + 8 * n) % nctx, y)),
    )

    def give(stage, total):
        buf, ssem, rsem, count, me, peer = stage
        buf[me] = total
        sends = []
        for n in range(1, count):
            ctx, heads = peer(n)
            sends.append(rcopy(buf.at[me], buf.at[me], ssem.at[n - 1], rsem.at[me], ctx, heads))
        for cp in sends:
            cp.start()
        return sends

    def collect(stage):
        buf, ssem, rsem, count, me, peer = stage
        for n in range(1, count):
            who = (me + n) % count
            rcopy(buf.at[who], buf.at[who], ssem.at[n - 1], rsem.at[who], c).wait_recv()
        return jnp.sum(buf[...], 0)

    given = give(stages[0], total)
    def passing(n):
        return rcopy(
            rbuf.at[n], red.at[0, h], fs_sem.at[n], pr_sem.at[0, h], zprev * 8 + 2 + n
        )

    def relay(places):
        @pl.when(x == 1)
        def _():
            for n in places:
                rcopy(pbuf.at[0], rbuf.at[n], ps_sem.at[0], rr_sem.at[n], c).wait_recv()
                passing(n).start()

    relay((0, 1))
    given += give(stages[1], collect(stages[0]))
    relay((2,))
    given += give(stages[2], collect(stages[1]))
    relay((3,))

    own_place = jnp.where(first, 4, x)

    def take(place, head):
        rcopy(
            pbuf.at[0], red.at[place, head], ps_sem.at[0], pr_sem.at[place, head], c
        ).wait_recv()

    take(own_place, 1 - h)
    acc[...] = red[own_place].astype(F32)
    for j in (3, 2, 1, 0):

        @pl.when(source & (True if j == 0 else j > x))
        def _():
            for hh in range(2):
                take(j, hh)
                acc[hh] += red[j, hh].astype(F32)

    for hh in range(2):
        dk = acc[hh, 0]
        un = dk * cosn[...] - pltpu.roll(dk, 64, 1) * sinn[...]
        normed = knorm[hh]
        gg = un * kg_ref[...]
        out = krec[hh] * (gg - normed * jnp.mean(gg * normed, -1, keepdims=True))
        dk_ref[:, hh * D : (hh + 1) * D] = out.astype(BF16)
        dv_ref[:, hh * D : (hh + 1) * D] = acc[hh, 1].astype(BF16)

    total = collect(stages[2])
    qgg_ref[...] = total[0:1]
    kgg_ref[...] = total[1:2]
    for cp in given:
        cp.wait_send()

    kv_sends(lambda cp: cp.wait_send())
    kv_on_chip.wait_send()
    auxc.wait_send()
    for cp in xc:
        cp.wait_send()

    def drain(slot, _):
        pl.when(slot != own_slot)(lambda: partial_copy(slot)[2].wait_send())
        return 0

    lax.fori_loop(0, slots, drain, 0)

    @pl.when(x == 1)
    def _():
        for n in range(4):
            passing(n).wait_send()

    dq_near.wait()
    dq_far.wait_send()
    dq_far.wait_recv()


def emit(dq, dk, dv, qg, kg, dq_out, dk_out, dv_out, qg_out, kg_out, big, small, isem, osem):
    pieces = [(dk, small.at[0], dk_out), (dv, small.at[1], dv_out)]
    for n in range(4):
        rows = pl.ds(n * 64, 64)
        pieces.append((dq.at[rows], big.at[rows], dq_out.at[rows]))
    ins = [pltpu.make_async_copy(a, b, isem.at[n]) for n, (a, b, _) in enumerate(pieces)]
    outs = [pltpu.make_async_copy(b, o, osem.at[n]) for n, (_, b, o) in enumerate(pieces)]
    for cp in ins:
        cp.start()
    qg_out[...] = qg[0]
    kg_out[...] = kg[0]
    for a, b in zip(ins, outs):
        a.wait()
        b.start()
    for b in outs:
        b.wait()


def on_device(nz, q_raw, k_raw, values, saved_out, out_grad, q_gain, k_gain, ancestors):
    lanes = np.arange(D) % (D // 2)
    freq = jnp.asarray(
        np.exp(lanes * (-2.0 * math.log(ROPE_BASE) / D)).astype(np.float32)[None, :]
    )
    vm = pl.BlockSpec(memory_space=pltpu.VMEM)
    hbm = pl.BlockSpec(memory_space=pl.ANY)
    V = pltpu.VMEM
    dma = pltpu.SemaphoreType.DMA
    outs = pl.pallas_call(
        functools.partial(kernel, nz),
        out_shape=(
            jax.ShapeDtypeStruct(q_raw.shape, BF16),
            jax.ShapeDtypeStruct(k_raw.shape, BF16),
            jax.ShapeDtypeStruct(k_raw.shape, BF16),
            jax.ShapeDtypeStruct((1, D), F32),
            jax.ShapeDtypeStruct((1, D), F32),
        ),
        in_specs=[hbm, vm, vm, hbm, hbm, vm, vm, vm, vm],
        out_specs=(hbm, vm, vm, vm, vm),
        scratch_shapes=[
            V((2, T, HALF), BF16), V((2, T, HALF), BF16), V((2, T, HALF), BF16),
            V((9, 2, T, D), BF16), V((2, 2, T, D), BF16), V((9, D, T), BF16),
            V((2, 160, T), F32), V((T, D), F32), V((T, D), F32),
            V((2, T, D), F32), V((2, T, D), F32),
            V((2, D, G * T), BF16), V((2, G, D, T), F32), V((2, G, 1, T), F32),
            V((2, D, G * T), BF16), V((2, G, 1, T), F32), V((2, G, D, T), F32),
            V((2, G, 1, T), F32), V((13, T, G * T), BF16), V((13, T, G * T), BF16),
            V((T, T), F32), V((T, T), BF16), V((2, T, D), F32),
            V((9, 2, T, D), BF16), V((4, 2, T, D), BF16), V((5, 2, 2, T, D), BF16), V((2, T, HALF), BF16),
            V((D, T), F32), V((1, D), F32), V((2, BLK, D), F32), V((2, 32, D), F32),
            V((2, 2, T, D), F32),
            V((8, 8, D), F32), V((4, 8, D), F32), V((nz, 8, D), F32),
            dma((3,)), dma((4,)), dma((4,)), dma((9,)), dma((9,)),
            dma((9,)), dma((5, 2)), dma((4,)), dma((4,)), dma, dma,
            dma((7,)), dma((8,)), dma((3,)), dma((4,)), dma((nz - 1,)), dma((nz,)),
        ],
        compiler_params=pltpu.CompilerParams(
            collective_id=0, has_side_effects=True, vmem_limit_bytes=63000000
        ),
    )(
        q_raw, k_raw, values, saved_out, out_grad,
        q_gain.reshape(1, D), k_gain.reshape(1, D), ancestors, freq,
    )
    return pl.pallas_call(
        emit,
        out_shape=(
            jax.ShapeDtypeStruct(q_raw.shape, BF16),
            jax.ShapeDtypeStruct(k_raw.shape, BF16),
            jax.ShapeDtypeStruct(k_raw.shape, BF16),
            jax.ShapeDtypeStruct((D,), F32),
            jax.ShapeDtypeStruct((D,), F32),
        ),
        in_specs=[hbm, hbm, hbm, vm, vm],
        out_specs=(hbm, hbm, hbm, vm, vm),
        scratch_shapes=[
            V(q_raw.shape, BF16), V((2,) + k_raw.shape, BF16), dma((6,)), dma((6,)),
        ],
    )(*outs)


def solution(mesh):
    nz = mesh.shape["ctx"] // 8
    wide = P("ctx", "heads")
    return jax.shard_map(
        functools.partial(on_device, nz),
        mesh=mesh,
        in_specs=(wide, wide, wide, wide, wide, P(), P(), P("ctx", None)),
        out_specs=(wide, wide, wide, P(), P()),
        check_vma=False,
    )
```

```python
import functools
import math

import jax
import jax.numpy as jnp
import numpy as np
from jax import lax
from jax.experimental import pallas as pl
from jax.experimental.pallas import tpu as pltpu
from jax.sharding import PartitionSpec as P

ROPE_BASE = 1000000.0
EPS = 1e-06
T = 256
D = 128
G = 8
BLK = 64
HALF = G * D
UNROLL = 8
INV_ROOT = 1.0 / math.sqrt(D)
EXP_SCALE = INV_ROOT * math.log2(math.e)
F32 = jnp.float32
BF16 = jnp.bfloat16


def nn(a, b):
    return lax.dot_general(a, b, (((1,), (0,)), ((), ())), preferred_element_type=F32)


def nt(a, b):
    return lax.dot_general(a, b, (((1,), (1,)), ((), ())), preferred_element_type=F32)


def kernel(
    nz, q_hbm, k_ref, v_ref, so_hbm, do_hbm, qg_ref, kg_ref, anc_ref, fr_ref,
    dq_hbm, dk_ref, dv_ref, qgg_ref, kgg_ref,
    qx, dox, sox, kv, kvs, kt, aux, cosn, sinn, knorm, krec,
    qrt, qnt, qr, dot, dos, dlt, dqt, esum, eb, gb, mask, eye, dkv, pbuf, rbuf, red, dqo,
    qga, kga, toff, tblk, acc, ar1, ar2, ar3,
    lsem, xs, xr, kvs_sem, kvr_sem, ps_sem, pr_sem, rr_sem, fs_sem, os_sem, or_sem,
    s1, r1, s2, r2, s3, r3,
):
    c = lax.axis_index("ctx")
    y = lax.axis_index("heads")
    z = c // 8
    x = (c % 8) // 2
    h = c % 2
    nctx = nz * 8
    znext = (z + 1) % nz
    zprev = (z + nz - 1) % nz
    partner = c + 1 - 2 * h
    first = x == 0

    def rcopy(src, dst, ssem, rsem, ctx, heads=None):
        return pltpu.make_async_remote_copy(
            src_ref=src, dst_ref=dst, send_sem=ssem, recv_sem=rsem,
            device_id=(ctx, y if heads is None else heads),
            device_id_type=pl.DeviceIdType.MESH,
        )

    mine = pl.ds(pl.multiple_of(h * HALF, HALF), HALF)
    other = pl.ds(pl.multiple_of((1 - h) * HALF, HALF), HALF)
    loads = [
        pltpu.make_async_copy(src.at[:, mine], dst.at[h], lsem.at[n])
        for n, (src, dst) in enumerate(((q_hbm, qx), (do_hbm, dox), (so_hbm, sox)))
    ]
    for cp in loads:
        cp.start()

    bar = pltpu.get_barrier_semaphore()

    def greet(ctx, heads=None):
        pl.semaphore_signal(
            bar, inc=1, device_id=(ctx, y if heads is None else heads),
            device_id_type=pl.DeviceIdType.MESH,
        )

    for n in range(1, 8):
        greet(z * 8 + (c % 8 + n) % 8)
    for n in range(1, 4):
        greet(c, (y + n) % 4)
    for n in range(1, nz):
        greet((c + 8 * n) % nctx)
    row = c % 8

    def greet_all(cond, base, places):
        @pl.when(cond)
        def _():
            for n in places:
                greet(base + n)

    greet_all(first, zprev * 8, range(1, 8))
    greet_all((row == 1) | (row >= 6), znext * 8, (0, 1))
    greet_all((row >= 2) & (row <= 5), znext * 8, (2, 3))
    greetings = (
        7 + 3 + nz - 1 + jnp.where(first, 3, 0) + jnp.where(x == 1, 4, 0) + jnp.where(row > 0, 2, 0)
    )

    anc = anc_ref[...]
    depth = jnp.sum((anc >= 0).astype(jnp.int32), axis=1, keepdims=True)
    off = lax.broadcasted_iota(jnp.int32, (BLK, D), 0)
    pos = jnp.concatenate(
        [(depth[b : b + 1] - 1) * BLK + off for b in range(4)], axis=0
    ).astype(F32)
    ang = pos * fr_ref[...]
    lane = lax.broadcasted_iota(jnp.int32, (T, D), 1)
    cos = jnp.cos(ang)
    sin = jnp.sin(ang)
    cosn[...] = cos
    sgn = jnp.where(lane < 64, -sin, sin)
    sinn[...] = sgn
    aux[h, 0:64, :] = cos.T[0:64]
    aux[h, 64:128, :] = sin.T[0:64]
    own_tree = jnp.where(first & (h == 0), zprev, z)
    ids = (lax.broadcasted_iota(jnp.int32, (32, 32), 0) + own_tree * 32 + 4) % (nz * 32)
    aux[h, 128:160, :] = jnp.concatenate(
        [
            jnp.broadcast_to(
                jnp.max(
                    jnp.where(jnp.broadcast_to(anc[b : b + 1], (32, 32)) == ids, 1.0, 0.0),
                    axis=1, keepdims=True,
                ),
                (32, BLK),
            )
            for b in range(4)
        ],
        axis=1,
    )
    eye[...] = jnp.where(
        lax.broadcasted_iota(jnp.int32, (T, T), 0) == lax.broadcasted_iota(jnp.int32, (T, T), 1),
        1.0, 0.0,
    ).astype(BF16)
    own_slot = jnp.where(first, 7 + h, 2 * x - 1 + h)
    other_slot = jnp.where(first, 8 - h, 2 * x - h)
    for hh in range(2):
        kf = k_ref[:, hh * D : (hh + 1) * D].astype(F32)
        rec = lax.rsqrt(jnp.mean(kf * kf, -1, keepdims=True) + EPS)
        normed = kf * rec
        scaled = normed * kg_ref[...]
        knorm[hh] = normed
        krec[hh] = jnp.broadcast_to(rec, (T, D))
        kvs[hh, 0] = (scaled * cos + pltpu.roll(scaled, 64, 1) * sgn).astype(BF16)
        kvs[hh, 1] = v_ref[:, hh * D : (hh + 1) * D]
    kv[own_slot] = kvs[h]
    dqt[...] = jnp.zeros_like(dqt)
    esum[...] = jnp.zeros_like(esum)
    qga[...] = jnp.zeros_like(qga)
    kga[...] = jnp.zeros_like(kga)
    sign = jnp.where(lane[0:1] < 64, -1.0, 1.0)
    ang_off = off.astype(F32) * fr_ref[...]
    toff[0] = jnp.cos(ang_off)
    toff[1] = jnp.sin(ang_off) * sign

    gain = jnp.broadcast_to(qg_ref[...], (D, D)).T[:, 0:1]

    def prep(dev):
        tab_c = aux[dev, 0:64, :]
        tab_s = aux[dev, 64:128, :]
        ones = jnp.ones((8, D), BF16)

        def head(g):
            cols = slice(g * D, (g + 1) * D)
            rows = slice(g * T, (g + 1) * T)
            qt = nt(eye[0:D, 0:D], qx[dev, :, cols])
            rec = lax.rsqrt(jnp.mean(qt * qt, 0, keepdims=True) + EPS)
            normed = qt * rec
            qnt[dev, g] = normed
            qr[dev, g] = rec
            scaled = normed * gain
            a, b = scaled[0:64], scaled[64:128]
            qrt[dev, :, rows] = jnp.concatenate(
                [a * tab_c - b * tab_s, b * tab_c + a * tab_s], 0
            ).astype(BF16)
            grad = dox[dev, :, cols]
            dot[dev, :, rows] = nt(eye[0:D, 0:D], grad).astype(BF16)
            prod = grad.astype(F32) * sox[dev, :, cols].astype(F32)
            hi = prod.astype(BF16)
            lo = (prod - hi.astype(F32)).astype(BF16)
            dlt[dev, g] = (nt(ones, hi) + nt(ones, lo))[0:1]

        for g in range(G):
            head(g)

    def unit(order):
        early = order <= 1
        swapped = jnp.where(early, jnp.where(order == 0, 1 - h, h), order)
        slot = jnp.where(first, 8 - swapped, 2 * x - (swapped + 1) // 2)
        dev = jnp.where(first, jnp.where(swapped == 0, 1, 0), 1 - swapped % 2)
        return dev, slot, swapped

    def arrive(slot, n):
        rcopy(
            kvs.at[0, n], kv.at[slot, n], kvs_sem.at[n, 0], kvr_sem.at[n, slot], c
        ).wait_recv()

    def tiles(dev, slot, store, masked):
        def heads(step, _):
            keys = kv[slot, 0]
            for u in range(UNROLL):
                g = step * UNROLL + u
                rows = pl.ds(pl.multiple_of(g * T, T), T)
                e = jnp.exp2(nn(keys, qrt[dev, :, rows]) * EXP_SCALE)
                if masked:
                    e = e * mask[...]
                eb[store, :, rows] = e.astype(BF16)
                esum[dev, g] += jnp.sum(e, 0, keepdims=True)
            return 0

        lax.fori_loop(0, G // UNROLL, heads, 0)

    def grad_tiles(dev, slot, store):
        def heads(step, _):
            vals, keys_t = kv[slot, 1], kt[slot]
            low = []
            for u in range(UNROLL):
                g = step * UNROLL + u
                rows = pl.ds(pl.multiple_of(g * T, T), T)
                dp = nn(vals, dot[dev, :, rows])
                gg = (eb[store, :, rows].astype(F32) * (dp - dlt[dev, g])).astype(BF16)
                low.append((g, rows, gg))
            for g, rows, gg in low:
                gb[store, :, rows] = gg
            for g, rows, gg in low:
                dqt[dev, g] += nn(keys_t, gg)
            return 0

        lax.fori_loop(0, G // UNROLL, heads, 0)

    def transpose_keys(slot):
        kt[slot] = nt(eye[0:D, 0:D], kv[slot, 0]).astype(BF16)

    def fill_mask(dev, index, causal):
        key = lax.broadcasted_iota(jnp.int32, (BLK, T), 0)
        tok = lax.broadcasted_iota(jnp.int32, (BLK, T), 1)
        for j in range(4):
            row = jnp.broadcast_to(aux[dev, pl.ds(128 + 4 * index + j, 1), :], (BLK, T))
            if causal:
                row = jnp.where(key + j * BLK <= tok, row, 0.0)
            mask[j * BLK : (j + 1) * BLK, :] = row

    def own_unit(order):
        dev, slot, store = unit(order)
        transpose_keys(slot)
        fill_mask(dev, jnp.where(slot == 8, 0, slot), True)
        tiles(dev, slot, store, True)

    for cp in loads:
        cp.wait()
    prep(h)
    own_unit(0)

    pl.semaphore_wait(bar, greetings)

    kv_on_chip = [
        rcopy(
            kvs.at[1 - h, n], kv.at[own_slot, n], kvs_sem.at[n, 8], kvr_sem.at[n, own_slot], partner
        )
        for n in range(2)
    ]
    xc = [
        rcopy(src.at[:, other], dst.at[h], xs.at[n], xr.at[n], partner)
        for n, (src, dst) in enumerate(((q_hbm, qx), (do_hbm, dox), (so_hbm, sox)))
    ]
    auxc = rcopy(aux.at[h], aux.at[h], xs.at[3], xr.at[3], partner)
    kv_on_chip[0].start()
    auxc.start()
    for cp in xc:
        cp.start()

    source = ~(first & (h == 0))
    position = jnp.where(first, 0, 2 * x - 1 + h)

    def kv_sends(act):
        for n in range(2):
            for j in range(4):
                dest = znext * 8 if j == 0 else z * 8 + 2 * j
                ok = source & (True if j == 0 else j > x)

                @pl.when(ok)
                def _():
                    for hh in range(2):
                        act(
                            rcopy(
                                kvs.at[hh, n], kv.at[position, n], kvs_sem.at[n, 2 * j + hh],
                                kvr_sem.at[n, position], dest + hh,
                            )
                        )

    kv_sends(lambda cp: cp.start())
    kv_on_chip[1].start()

    auxc.wait_recv()
    for cp in xc:
        cp.wait_recv()
    prep(1 - h)
    arrive(other_slot, 0)
    own_unit(1)

    tri = jnp.where(
        lax.broadcasted_iota(jnp.int32, (32, 32), 0) >= lax.broadcasted_iota(jnp.int32, (32, 32), 1),
        1.0, 0.0,
    ).astype(BF16)
    count = jnp.ones((32, 1), F32)
    for dev in range(2):
        seen = aux[dev, 128:160, :]
        upto = nn(tri, seen.astype(BF16))
        count = jnp.maximum(count, jnp.max(seen * upto, axis=1, keepdims=True))
    ang_blk = jnp.broadcast_to((count - 1.0) * BLK, (32, D)) * fr_ref[...]
    tblk[0] = jnp.cos(ang_blk)
    tblk[1] = jnp.sin(ang_blk) * sign

    units = jnp.where(first, 9, 4 * x + 1)

    def later(order, _):
        dev, slot, store = unit(order)

        @pl.when(first | (order % 2 == 1))
        def _():
            arrive(slot, 0)
            transpose_keys(slot)

        @pl.when(slot >= 4)
        def _():
            fill_mask(dev, slot, False)
            tiles(dev, slot, store, True)

        pl.when(slot < 4)(lambda: tiles(dev, slot, store, False))
        return 0

    lax.fori_loop(2, units, later, 0)

    def finish(dev):
        tab_c = aux[dev, 0:64, :]
        tab_s = aux[dev, 64:128, :]
        part = jnp.zeros((D, T), F32)
        for g in range(G):
            up = dqt[dev, g] * (esum[dev, g] * INV_ROOT)
            a, b = up[0:64], up[64:128]
            un = jnp.concatenate([a * tab_c + b * tab_s, b * tab_c - a * tab_s], 0)
            normed = qnt[dev, g]
            part += un * normed
            gg = un * gain
            dq = qr[dev, g] * (gg - normed * jnp.mean(gg * normed, 0, keepdims=True))
            dqo[dev, :, g * D : (g + 1) * D] = nt(eye[...], dq.astype(BF16)).astype(BF16)
        qga[...] += part

    def normalise(dev):
        for g in range(G):
            rows = slice(g * T, (g + 1) * T)
            inv = 1.0 / esum[dev, g]
            esum[dev, g] = inv
            qrt[dev, :, rows] = (qrt[dev, :, rows].astype(F32) * (inv * INV_ROOT)).astype(BF16)
            dos[dev, :, rows] = (dot[dev, :, rows].astype(F32) * inv).astype(BF16)

    for dev in range(2):
        normalise(dev)

    slots = jnp.where(first, 9, 2 * x + 1)

    def partial_copy(slot):
        owner = jnp.where(
            first & (slot < 8), zprev * 8 + 1 + slot, z * 8 + 1 + jnp.where(slot == 8, 0, slot)
        ) % nctx
        place = jnp.where(first & (slot >= 7), 4, x)
        cp = rcopy(
            pbuf.at[slot], red.at[place, h], ps_sem.at[slot], pr_sem.at[place, h], owner
        )
        return owner, place, cp

    def second_pass(step, _):
        slot = step
        dev = jnp.where(first & (slot < 8), 0, 1)
        store = jnp.where(first, 8 - slot, 2 * (2 * x - slot))
        pl.when(slot != own_slot)(lambda: arrive(slot, 1))
        grad_tiles(dev, slot, store)
        dkv[0] = nt(gb[store], qrt[dev])
        dkv[1] = nt(eb[store], dos[dev])

        @pl.when(jnp.logical_not(first) & (slot < 2 * x))
        def _():
            grad_tiles(0, slot, store - 1)
            dkv[0] += nt(gb[store - 1], qrt[0])
            dkv[1] += nt(eb[store - 1], dos[0])

        pbuf[slot] = dkv[...].astype(BF16)
        gains = jnp.zeros((1, D), F32)
        for j in range(4):
            place = pl.ds(4 * jnp.where(slot == 8, 0, slot) + j, 1)
            part = slice(j * BLK, (j + 1) * BLK)
            cos_b, sin_b = tblk[0, place, :], tblk[1, place, :]
            cos_k = cos_b * toff[0] - sin_b * toff[1]
            sin_k = sin_b * toff[0] + cos_b * toff[1]
            dkp = dkv[0, part]
            key = kv[slot, 0, part].astype(F32)
            gains += jnp.sum(
                (dkp * cos_k - pltpu.roll(dkp, 64, 1) * sin_k)
                * (key * cos_k - pltpu.roll(key, 64, 1) * sin_k),
                0, keepdims=True,
            )
        kga[...] += gains
        owner, place, cp = partial_copy(slot)

        @pl.when(slot == own_slot)
        def _():
            red[place, h] = pbuf[slot]

        far = first & (slot >= 1) & (slot <= 4)
        pl.when((slot != own_slot) & jnp.logical_not(far))(lambda: cp.start())

        @pl.when(far)
        def _():
            place = jnp.clip(slot - 1, 0, 3)
            rcopy(
                pbuf.at[slot], rbuf.at[place], ps_sem.at[slot], rr_sem.at[place], z * 8 + 2 + h
            ).start()

        return 0

    lax.fori_loop(0, slots, second_pass, 0)

    finish(1 - h)
    dq_far = rcopy(dqo.at[1 - h], dq_hbm.at[:, mine], os_sem, or_sem, partner)
    dq_far.start()
    finish(h)
    dq_near = pltpu.make_async_copy(dqo.at[h], dq_hbm.at[:, mine], lsem.at[0])
    dq_near.start()

    qcol = jnp.broadcast_to(jnp.sum(qga[...], 1, keepdims=True), (D, D)).T
    sub = lax.broadcasted_iota(jnp.int32, (8, D), 0)
    ksum = jnp.broadcast_to(kga[...] / kg_ref[...], (8, D))
    total = jnp.where(sub == 0, qcol[0:8], jnp.where(sub == 1, ksum, 0.0))
    stages = (
        (ar1, s1, r1, 8, c % 8, lambda n: (z * 8 + (c % 8 + n) % 8, y)),
        (ar2, s2, r2, 4, y, lambda n: (c, (y + n) % 4)),
        (ar3, s3, r3, nz, z, lambda n: ((c + 8 * n) % nctx, y)),
    )

    def give(stage, total):
        buf, ssem, rsem, count, me, peer = stage
        buf[me] = total
        sends = []
        for n in range(1, count):
            ctx, heads = peer(n)
            sends.append(rcopy(buf.at[me], buf.at[me], ssem.at[n - 1], rsem.at[me], ctx, heads))
        for cp in sends:
            cp.start()
        return sends

    def collect(stage):
        buf, ssem, rsem, count, me, peer = stage
        for n in range(1, count):
            who = (me + n) % count
            rcopy(buf.at[who], buf.at[who], ssem.at[n - 1], rsem.at[who], c).wait_recv()
        return jnp.sum(buf[...], 0)

    given = give(stages[0], total)
    def passing(n):
        return rcopy(
            rbuf.at[n], red.at[0, h], fs_sem.at[n], pr_sem.at[0, h], zprev * 8 + 2 + n
        )

    def relay(places):
        @pl.when(x == 1)
        def _():
            for n in places:
                rcopy(pbuf.at[0], rbuf.at[n], ps_sem.at[0], rr_sem.at[n], c).wait_recv()
                passing(n).start()

    relay((0, 1))
    given += give(stages[1], collect(stages[0]))
    relay((2,))
    given += give(stages[2], collect(stages[1]))
    relay((3,))

    own_place = jnp.where(first, 4, x)

    def take(place, head):
        rcopy(
            pbuf.at[0], red.at[place, head], ps_sem.at[0], pr_sem.at[place, head], c
        ).wait_recv()

    take(own_place, 1 - h)
    acc[...] = red[own_place].astype(F32)
    for j in (3, 2, 1, 0):

        @pl.when(source & (True if j == 0 else j > x))
        def _():
            for hh in range(2):
                take(j, hh)
                acc[hh] += red[j, hh].astype(F32)

    for hh in range(2):
        dk = acc[hh, 0]
        un = dk * cosn[...] - pltpu.roll(dk, 64, 1) * sinn[...]
        normed = knorm[hh]
        gg = un * kg_ref[...]
        out = krec[hh] * (gg - normed * jnp.mean(gg * normed, -1, keepdims=True))
        dk_ref[:, hh * D : (hh + 1) * D] = out.astype(BF16)
        dv_ref[:, hh * D : (hh + 1) * D] = acc[hh, 1].astype(BF16)

    total = collect(stages[2])
    qgg_ref[...] = total[0:1]
    kgg_ref[...] = total[1:2]
    for cp in given:
        cp.wait_send()

    kv_sends(lambda cp: cp.wait_send())
    for cp in kv_on_chip:
        cp.wait_send()
    auxc.wait_send()
    for cp in xc:
        cp.wait_send()

    def drain(slot, _):
        pl.when(slot != own_slot)(lambda: partial_copy(slot)[2].wait_send())
        return 0

    lax.fori_loop(0, slots, drain, 0)

    @pl.when(x == 1)
    def _():
        for n in range(4):
            passing(n).wait_send()

    dq_near.wait()
    dq_far.wait_send()
    dq_far.wait_recv()


def emit(dq, dk, dv, qg, kg, dq_out, dk_out, dv_out, qg_out, kg_out, big, small, isem, osem):
    pieces = [(dk, small.at[0], dk_out), (dv, small.at[1], dv_out)]
    for n in range(4):
        rows = pl.ds(n * 64, 64)
        pieces.append((dq.at[rows], big.at[rows], dq_out.at[rows]))
    ins = [pltpu.make_async_copy(a, b, isem.at[n]) for n, (a, b, _) in enumerate(pieces)]
    outs = [pltpu.make_async_copy(b, o, osem.at[n]) for n, (_, b, o) in enumerate(pieces)]
    for cp in ins:
        cp.start()
    qg_out[...] = qg[0]
    kg_out[...] = kg[0]
    for a, b in zip(ins, outs):
        a.wait()
        b.start()
    for b in outs:
        b.wait()


def on_device(nz, q_raw, k_raw, values, saved_out, out_grad, q_gain, k_gain, ancestors):
    lanes = np.arange(D) % (D // 2)
    freq = jnp.asarray(
        np.exp(lanes * (-2.0 * math.log(ROPE_BASE) / D)).astype(np.float32)[None, :]
    )
    vm = pl.BlockSpec(memory_space=pltpu.VMEM)
    hbm = pl.BlockSpec(memory_space=pl.ANY)
    V = pltpu.VMEM
    dma = pltpu.SemaphoreType.DMA
    outs = pl.pallas_call(
        functools.partial(kernel, nz),
        out_shape=(
            jax.ShapeDtypeStruct(q_raw.shape, BF16),
            jax.ShapeDtypeStruct(k_raw.shape, BF16),
            jax.ShapeDtypeStruct(k_raw.shape, BF16),
            jax.ShapeDtypeStruct((1, D), F32),
            jax.ShapeDtypeStruct((1, D), F32),
        ),
        in_specs=[hbm, vm, vm, hbm, hbm, vm, vm, vm, vm],
        out_specs=(hbm, vm, vm, vm, vm),
        scratch_shapes=[
            V((2, T, HALF), BF16), V((2, T, HALF), BF16), V((2, T, HALF), BF16),
            V((9, 2, T, D), BF16), V((2, 2, T, D), BF16), V((9, D, T), BF16),
            V((2, 160, T), F32), V((T, D), F32), V((T, D), F32),
            V((2, T, D), F32), V((2, T, D), F32),
            V((2, D, G * T), BF16), V((2, G, D, T), F32), V((2, G, 1, T), F32),
            V((2, D, G * T), BF16), V((2, D, G * T), BF16), V((2, G, 1, T), F32), V((2, G, D, T), F32),
            V((2, G, 1, T), F32), V((13, T, G * T), BF16), V((13, T, G * T), BF16),
            V((T, T), F32), V((T, T), BF16), V((2, T, D), F32),
            V((9, 2, T, D), BF16), V((4, 2, T, D), BF16), V((5, 2, 2, T, D), BF16), V((2, T, HALF), BF16),
            V((D, T), F32), V((1, D), F32), V((2, BLK, D), F32), V((2, 32, D), F32),
            V((2, 2, T, D), F32),
            V((8, 8, D), F32), V((4, 8, D), F32), V((nz, 8, D), F32),
            dma((3,)), dma((4,)), dma((4,)), dma((2, 9)), dma((2, 9)),
            dma((9,)), dma((5, 2)), dma((4,)), dma((4,)), dma, dma,
            dma((7,)), dma((8,)), dma((3,)), dma((4,)), dma((nz - 1,)), dma((nz,)),
        ],
        compiler_params=pltpu.CompilerParams(
            collective_id=0, has_side_effects=True, vmem_limit_bytes=63000000
        ),
    )(
        q_raw, k_raw, values, saved_out, out_grad,
        q_gain.reshape(1, D), k_gain.reshape(1, D), ancestors, freq,
    )
    return pl.pallas_call(
        emit,
        out_shape=(
            jax.ShapeDtypeStruct(q_raw.shape, BF16),
            jax.ShapeDtypeStruct(k_raw.shape, BF16),
            jax.ShapeDtypeStruct(k_raw.shape, BF16),
            jax.ShapeDtypeStruct((D,), F32),
            jax.ShapeDtypeStruct((D,), F32),
        ),
        in_specs=[hbm, hbm, hbm, vm, vm],
        out_specs=(hbm, hbm, hbm, vm, vm),
        scratch_shapes=[
            V(q_raw.shape, BF16), V((2,) + k_raw.shape, BF16), dma((6,)), dma((6,)),
        ],
    )(*outs)


def solution(mesh):
    nz = mesh.shape["ctx"] // 8
    wide = P("ctx", "heads")
    return jax.shard_map(
        functools.partial(on_device, nz),
        mesh=mesh,
        in_specs=(wide, wide, wide, wide, wide, P(), P(), P("ctx", None)),
        out_specs=(wide, wide, wide, P(), P()),
        check_vma=False,
    )
```

```python
import functools
import math

import jax
import jax.numpy as jnp
import numpy as np
from jax import lax
from jax.experimental import pallas as pl
from jax.experimental.pallas import tpu as pltpu
from jax.sharding import PartitionSpec as P

ROPE_BASE = 1000000.0
EPS = 1e-06
T = 256
D = 128
G = 8
BLK = 64
HALF = G * D
UNROLL = 8
INV_ROOT = 1.0 / math.sqrt(D)
EXP_SCALE = INV_ROOT * math.log2(math.e)
F32 = jnp.float32
BF16 = jnp.bfloat16


def nn(a, b):
    return lax.dot_general(a, b, (((1,), (0,)), ((), ())), preferred_element_type=F32)


def nt(a, b):
    return lax.dot_general(a, b, (((1,), (1,)), ((), ())), preferred_element_type=F32)


def kernel(
    nz, q_hbm, k_ref, v_ref, so_hbm, do_hbm, qg_ref, kg_ref, anc_ref, fr_ref,
    dq_hbm, dk_ref, dv_ref, qgg_ref, kgg_ref,
    qx, dox, sox, kv, kvs, kt, aux, cosn, sinn, knorm, krec,
    qrt, qnt, qr, dot, dos, dlt, dqt, esum, eb, gb, mask, eye, dkv, pbuf, rbuf, red, dqo,
    qga, kga, toff, tblk, acc, ar1, ar2, ar3,
    lsem, xs, xr, kvs_sem, kvr_sem, ps_sem, pr_sem, rr_sem, fs_sem, os_sem, or_sem,
    s1, r1, s2, r2, s3, r3,
):
    c = lax.axis_index("ctx")
    y = lax.axis_index("heads")
    z = c // 8
    x = (c % 8) // 2
    h = c % 2
    nctx = nz * 8
    znext = (z + 1) % nz
    zprev = (z + nz - 1) % nz
    partner = c + 1 - 2 * h
    first = x == 0

    def rcopy(src, dst, ssem, rsem, ctx, heads=None):
        return pltpu.make_async_remote_copy(
            src_ref=src, dst_ref=dst, send_sem=ssem, recv_sem=rsem,
            device_id=(ctx, y if heads is None else heads),
            device_id_type=pl.DeviceIdType.MESH,
        )

    mine = pl.ds(pl.multiple_of(h * HALF, HALF), HALF)
    other = pl.ds(pl.multiple_of((1 - h) * HALF, HALF), HALF)
    loads = [
        pltpu.make_async_copy(src.at[:, mine], dst.at[h], lsem.at[n])
        for n, (src, dst) in enumerate(((q_hbm, qx), (do_hbm, dox), (so_hbm, sox)))
    ]
    for cp in loads:
        cp.start()

    bar = pltpu.get_barrier_semaphore()

    def greet(ctx, heads=None):
        pl.semaphore_signal(
            bar, inc=1, device_id=(ctx, y if heads is None else heads),
            device_id_type=pl.DeviceIdType.MESH,
        )

    for n in range(1, 8):
        greet(z * 8 + (c % 8 + n) % 8)
    for n in range(1, 4):
        greet(c, (y + n) % 4)
    for n in range(1, nz):
        greet((c + 8 * n) % nctx)
    row = c % 8

    def greet_all(cond, base, places):
        @pl.when(cond)
        def _():
            for n in places:
                greet(base + n)

    greet_all(first, zprev * 8, range(1, 8))
    greet_all((row == 1) | (row >= 6), znext * 8, (0, 1))
    greet_all((row >= 2) & (row <= 5), znext * 8, (2, 3))
    greetings = (
        7 + 3 + nz - 1 + jnp.where(first, 3, 0) + jnp.where(x == 1, 4, 0) + jnp.where(row > 0, 2, 0)
    )

    anc = anc_ref[...]
    depth = jnp.sum((anc >= 0).astype(jnp.int32), axis=1, keepdims=True)
    off = lax.broadcasted_iota(jnp.int32, (BLK, D), 0)
    pos = jnp.concatenate(
        [(depth[b : b + 1] - 1) * BLK + off for b in range(4)], axis=0
    ).astype(F32)
    ang = pos * fr_ref[...]
    lane = lax.broadcasted_iota(jnp.int32, (T, D), 1)
    cos = jnp.cos(ang)
    sin = jnp.sin(ang)
    cosn[...] = cos
    sgn = jnp.where(lane < 64, -sin, sin)
    sinn[...] = sgn
    aux[h, 0:64, :] = cos.T[0:64]
    aux[h, 64:128, :] = sin.T[0:64]
    own_tree = jnp.where(first & (h == 0), zprev, z)
    ids = (lax.broadcasted_iota(jnp.int32, (32, 32), 0) + own_tree * 32 + 4) % (nz * 32)
    aux[h, 128:160, :] = jnp.concatenate(
        [
            jnp.broadcast_to(
                jnp.max(
                    jnp.where(jnp.broadcast_to(anc[b : b + 1], (32, 32)) == ids, 1.0, 0.0),
                    axis=1, keepdims=True,
                ),
                (32, BLK),
            )
            for b in range(4)
        ],
        axis=1,
    )
    eye[...] = jnp.where(
        lax.broadcasted_iota(jnp.int32, (T, T), 0) == lax.broadcasted_iota(jnp.int32, (T, T), 1),
        1.0, 0.0,
    ).astype(BF16)
    own_slot = jnp.where(first, 7 + h, 2 * x - 1 + h)
    other_slot = jnp.where(first, 8 - h, 2 * x - h)
    for hh in range(2):
        kf = k_ref[:, hh * D : (hh + 1) * D].astype(F32)
        rec = lax.rsqrt(jnp.mean(kf * kf, -1, keepdims=True) + EPS)
        normed = kf * rec
        scaled = normed * kg_ref[...]
        knorm[hh] = normed
        krec[hh] = jnp.broadcast_to(rec, (T, D))
        kvs[hh, 0] = (scaled * cos + pltpu.roll(scaled, 64, 1) * sgn).astype(BF16)
        kvs[hh, 1] = v_ref[:, hh * D : (hh + 1) * D]
    kv[own_slot] = kvs[h]
    dqt[...] = jnp.zeros_like(dqt)
    esum[...] = jnp.zeros_like(esum)
    qga[...] = jnp.zeros_like(qga)
    kga[...] = jnp.zeros_like(kga)
    sign = jnp.where(lane[0:1] < 64, -1.0, 1.0)
    ang_off = off.astype(F32) * fr_ref[...]
    toff[0] = jnp.cos(ang_off)
    toff[1] = jnp.sin(ang_off) * sign

    gain = jnp.broadcast_to(qg_ref[...], (D, D)).T[:, 0:1]

    def prep(dev):
        tab_c = aux[dev, 0:64, :]
        tab_s = aux[dev, 64:128, :]
        ones = jnp.ones((8, D), BF16)

        def head(g):
            cols = slice(g * D, (g + 1) * D)
            rows = slice(g * T, (g + 1) * T)
            qt = nt(eye[0:D, 0:D], qx[dev, :, cols])
            rec = lax.rsqrt(jnp.mean(qt * qt, 0, keepdims=True) + EPS)
            normed = qt * rec
            qnt[dev, g] = normed
            qr[dev, g] = rec
            scaled = normed * gain
            a, b = scaled[0:64], scaled[64:128]
            qrt[dev, :, rows] = jnp.concatenate(
                [a * tab_c - b * tab_s, b * tab_c + a * tab_s], 0
            ).astype(BF16)
            grad = dox[dev, :, cols]
            dot[dev, :, rows] = nt(eye[0:D, 0:D], grad).astype(BF16)
            prod = grad.astype(F32) * sox[dev, :, cols].astype(F32)
            hi = prod.astype(BF16)
            lo = (prod - hi.astype(F32)).astype(BF16)
            dlt[dev, g] = (nt(ones, hi) + nt(ones, lo))[0:1]

        for g in range(G):
            head(g)

    def unit(order):
        early = order <= 1
        swapped = jnp.where(early, jnp.where(order == 0, 1 - h, h), order)
        slot = jnp.where(first, 8 - swapped, 2 * x - (swapped + 1) // 2)
        dev = jnp.where(first, jnp.where(swapped == 0, 1, 0), 1 - swapped % 2)
        return dev, slot, swapped

    def arrive(slot, n):
        rcopy(
            kvs.at[0, n], kv.at[slot, n], kvs_sem.at[n, 0], kvr_sem.at[n, slot], c
        ).wait_recv()

    def tiles(dev, slot, store, masked):
        def heads(step, _):
            keys = kv[slot, 0]
            for u in range(UNROLL):
                g = step * UNROLL + u
                rows = pl.ds(pl.multiple_of(g * T, T), T)
                e = jnp.exp2(nn(keys, qrt[dev, :, rows]) * EXP_SCALE)
                if masked:
                    e = e * mask[...]
                eb[store, :, rows] = e.astype(BF16)
                esum[dev, g] += jnp.sum(e, 0, keepdims=True)
            return 0

        lax.fori_loop(0, G // UNROLL, heads, 0)

    def grad_tiles(dev, slot, store):
        def heads(step, _):
            vals, keys_t = kv[slot, 1], kt[slot]
            low = []
            for u in range(UNROLL):
                g = step * UNROLL + u
                rows = pl.ds(pl.multiple_of(g * T, T), T)
                dp = nn(vals, dot[dev, :, rows])
                gg = (eb[store, :, rows].astype(F32) * (dp - dlt[dev, g])).astype(BF16)
                low.append((g, rows, gg))
            for g, rows, gg in low:
                gb[store, :, rows] = gg
            for g, rows, gg in low:
                dqt[dev, g] += nn(keys_t, gg)
            return 0

        lax.fori_loop(0, G // UNROLL, heads, 0)

    def transpose_keys(slot):
        kt[slot] = nt(eye[0:D, 0:D], kv[slot, 0]).astype(BF16)

    def fill_mask(dev, index, causal):
        key = lax.broadcasted_iota(jnp.int32, (BLK, T), 0)
        tok = lax.broadcasted_iota(jnp.int32, (BLK, T), 1)
        for j in range(4):
            row = jnp.broadcast_to(aux[dev, pl.ds(128 + 4 * index + j, 1), :], (BLK, T))
            if causal:
                row = jnp.where(key + j * BLK <= tok, row, 0.0)
            mask[j * BLK : (j + 1) * BLK, :] = row

    def own_unit(order):
        dev, slot, store = unit(order)
        transpose_keys(slot)
        fill_mask(dev, jnp.where(slot == 8, 0, slot), True)
        tiles(dev, slot, store, True)

    for cp in loads:
        cp.wait()
    prep(h)
    own_unit(0)

    pl.semaphore_wait(bar, greetings)

    kv_on_chip = [
        rcopy(
            kvs.at[1 - h, n], kv.at[own_slot, n], kvs_sem.at[n, 8], kvr_sem.at[n, own_slot], partner
        )
        for n in range(2)
    ]
    xc = [
        rcopy(src.at[:, other], dst.at[h], xs.at[n], xr.at[n], partner)
        for n, (src, dst) in enumerate(((q_hbm, qx), (do_hbm, dox), (so_hbm, sox)))
    ]
    auxc = rcopy(aux.at[h], aux.at[h], xs.at[3], xr.at[3], partner)
    kv_on_chip[0].start()
    auxc.start()
    for cp in xc:
        cp.start()

    source = ~(first & (h == 0))
    position = jnp.where(first, 0, 2 * x - 1 + h)

    def kv_sends(act):
        for n in range(2):
            for j in range(4):
                dest = znext * 8 if j == 0 else z * 8 + 2 * j
                ok = source & (True if j == 0 else j > x)

                @pl.when(ok)
                def _():
                    for hh in range(2):
                        act(
                            rcopy(
                                kvs.at[hh, n], kv.at[position, n], kvs_sem.at[n, 2 * j + hh],
                                kvr_sem.at[n, position], dest + hh,
                            )
                        )

    kv_sends(lambda cp: cp.start())
    kv_on_chip[1].start()

    auxc.wait_recv()
    for cp in xc:
        cp.wait_recv()
    prep(1 - h)
    arrive(other_slot, 0)
    own_unit(1)

    tri = jnp.where(
        lax.broadcasted_iota(jnp.int32, (32, 32), 0) >= lax.broadcasted_iota(jnp.int32, (32, 32), 1),
        1.0, 0.0,
    ).astype(BF16)
    count = jnp.ones((32, 1), F32)
    for dev in range(2):
        seen = aux[dev, 128:160, :]
        upto = nn(tri, seen.astype(BF16))
        count = jnp.maximum(count, jnp.max(seen * upto, axis=1, keepdims=True))
    ang_blk = jnp.broadcast_to((count - 1.0) * BLK, (32, D)) * fr_ref[...]
    tblk[0] = jnp.cos(ang_blk)
    tblk[1] = jnp.sin(ang_blk) * sign

    units = jnp.where(first, 9, 4 * x + 1)

    def later(order, _):
        dev, slot, store = unit(order)

        @pl.when(first | (order % 2 == 1))
        def _():
            arrive(slot, 0)
            transpose_keys(slot)

        @pl.when(slot >= 4)
        def _():
            fill_mask(dev, slot, False)
            tiles(dev, slot, store, True)

        pl.when(slot < 4)(lambda: tiles(dev, slot, store, False))
        return 0

    lax.fori_loop(2, units, later, 0)

    def finish(dev):
        tab_c = aux[dev, 0:64, :]
        tab_s = aux[dev, 64:128, :]
        part = jnp.zeros((D, T), F32)
        for g in range(G):
            up = dqt[dev, g] * (esum[dev, g] * INV_ROOT)
            a, b = up[0:64], up[64:128]
            un = jnp.concatenate([a * tab_c + b * tab_s, b * tab_c - a * tab_s], 0)
            normed = qnt[dev, g]
            part += un * normed
            gg = un * gain
            dq = qr[dev, g] * (gg - normed * jnp.mean(gg * normed, 0, keepdims=True))
            dqo[dev, :, g * D : (g + 1) * D] = nt(eye[...], dq.astype(BF16)).astype(BF16)
        qga[...] += part

    def normalise(dev):
        for g in range(G):
            rows = slice(g * T, (g + 1) * T)
            inv = 1.0 / esum[dev, g]
            esum[dev, g] = inv
            qrt[dev, :, rows] = (qrt[dev, :, rows].astype(F32) * (inv * INV_ROOT)).astype(BF16)
            dos[dev, :, rows] = (dot[dev, :, rows].astype(F32) * inv).astype(BF16)

    for dev in range(2):
        normalise(dev)

    slots = jnp.where(first, 9, 2 * x + 1)

    def partial_copy(slot, n):
        owner = jnp.where(
            first & (slot < 8), zprev * 8 + 1 + slot, z * 8 + 1 + jnp.where(slot == 8, 0, slot)
        ) % nctx
        place = jnp.where(first & (slot >= 7), 4, x)
        cp = rcopy(
            pbuf.at[slot, n], red.at[place, h, n], ps_sem.at[n, slot], pr_sem.at[n, place, h], owner
        )
        return owner, place, cp

    def deliver(slot, n):
        owner, place, cp = partial_copy(slot, n)

        @pl.when(slot == own_slot)
        def _():
            red[place, h, n] = pbuf[slot, n]

        far = first & (slot >= 1) & (slot <= 4)
        pl.when((slot != own_slot) & jnp.logical_not(far))(lambda: cp.start())

        @pl.when(far)
        def _():
            place = jnp.clip(slot - 1, 0, 3)
            rcopy(
                pbuf.at[slot, n], rbuf.at[place, n], ps_sem.at[n, slot], rr_sem.at[n, place],
                z * 8 + 2 + h,
            ).start()

    def second_pass(step, _):
        slot = step
        dev = jnp.where(first & (slot < 8), 0, 1)
        store = jnp.where(first, 8 - slot, 2 * (2 * x - slot))
        pl.when(slot != own_slot)(lambda: arrive(slot, 1))
        grad_tiles(dev, slot, store)
        dkv[0] = nt(gb[store], qrt[dev])

        @pl.when(jnp.logical_not(first) & (slot < 2 * x))
        def _():
            grad_tiles(0, slot, store - 1)
            dkv[0] += nt(gb[store - 1], qrt[0])

        pbuf[slot, 0] = dkv[0].astype(BF16)
        gains = jnp.zeros((1, D), F32)
        for j in range(4):
            place = pl.ds(4 * jnp.where(slot == 8, 0, slot) + j, 1)
            part = slice(j * BLK, (j + 1) * BLK)
            cos_b, sin_b = tblk[0, place, :], tblk[1, place, :]
            cos_k = cos_b * toff[0] - sin_b * toff[1]
            sin_k = sin_b * toff[0] + cos_b * toff[1]
            dkp = dkv[0, part]
            key = kv[slot, 0, part].astype(F32)
            gains += jnp.sum(
                (dkp * cos_k - pltpu.roll(dkp, 64, 1) * sin_k)
                * (key * cos_k - pltpu.roll(key, 64, 1) * sin_k),
                0, keepdims=True,
            )
        kga[...] += gains
        deliver(slot, 0)
        return 0

    lax.fori_loop(0, slots, second_pass, 0)

    def value_pass(slot, _):
        dev = jnp.where(first & (slot < 8), 0, 1)
        store = jnp.where(first, 8 - slot, 2 * (2 * x - slot))
        dkv[1] = nt(eb[store], dos[dev])

        @pl.when(jnp.logical_not(first) & (slot < 2 * x))
        def _():
            dkv[1] += nt(eb[store - 1], dos[0])

        pbuf[slot, 1] = dkv[1].astype(BF16)
        deliver(slot, 1)
        return 0

    finish(1 - h)
    dq_far = rcopy(dqo.at[1 - h], dq_hbm.at[:, mine], os_sem, or_sem, partner)
    dq_far.start()
    finish(h)
    dq_near = pltpu.make_async_copy(dqo.at[h], dq_hbm.at[:, mine], lsem.at[0])
    dq_near.start()

    qcol = jnp.broadcast_to(jnp.sum(qga[...], 1, keepdims=True), (D, D)).T
    sub = lax.broadcasted_iota(jnp.int32, (8, D), 0)
    ksum = jnp.broadcast_to(kga[...] / kg_ref[...], (8, D))
    total = jnp.where(sub == 0, qcol[0:8], jnp.where(sub == 1, ksum, 0.0))
    stages = (
        (ar1, s1, r1, 8, c % 8, lambda n: (z * 8 + (c % 8 + n) % 8, y)),
        (ar2, s2, r2, 4, y, lambda n: (c, (y + n) % 4)),
        (ar3, s3, r3, nz, z, lambda n: ((c + 8 * n) % nctx, y)),
    )

    def give(stage, total):
        buf, ssem, rsem, count, me, peer = stage
        buf[me] = total
        sends = []
        for n in range(1, count):
            ctx, heads = peer(n)
            sends.append(rcopy(buf.at[me], buf.at[me], ssem.at[n - 1], rsem.at[me], ctx, heads))
        for cp in sends:
            cp.start()
        return sends

    def collect(stage):
        buf, ssem, rsem, count, me, peer = stage
        for n in range(1, count):
            who = (me + n) % count
            rcopy(buf.at[who], buf.at[who], ssem.at[n - 1], rsem.at[who], c).wait_recv()
        return jnp.sum(buf[...], 0)

    given = give(stages[0], total)
    def passing(m, n):
        return rcopy(
            rbuf.at[n, m], red.at[0, h, m], fs_sem.at[m, n], pr_sem.at[m, 0, h],
            zprev * 8 + 2 + n,
        )

    def relay(m, places):
        @pl.when(x == 1)
        def _():
            for n in places:
                rcopy(
                    pbuf.at[0, m], rbuf.at[n, m], ps_sem.at[m, 0], rr_sem.at[m, n], c
                ).wait_recv()
                passing(m, n).start()

    lax.fori_loop(0, jnp.minimum(slots, 3), value_pass, 0)
    relay(0, (0, 1, 2, 3))
    given += give(stages[1], collect(stages[0]))
    lax.fori_loop(3, jnp.minimum(slots, 6), value_pass, 0)
    relay(1, (0, 1))
    given += give(stages[2], collect(stages[1]))
    lax.fori_loop(6, slots, value_pass, 0)
    relay(1, (2, 3))

    own_place = jnp.where(first, 4, x)

    def take(place, head):
        for n in range(2):
            rcopy(
                pbuf.at[0, n], red.at[place, head, n], ps_sem.at[n, 0], pr_sem.at[n, place, head], c
            ).wait_recv()

    take(own_place, 1 - h)
    acc[...] = red[own_place].astype(F32)
    for j in (3, 2, 1, 0):

        @pl.when(source & (True if j == 0 else j > x))
        def _():
            for hh in range(2):
                take(j, hh)
                acc[hh] += red[j, hh].astype(F32)

    for hh in range(2):
        dk = acc[hh, 0]
        un = dk * cosn[...] - pltpu.roll(dk, 64, 1) * sinn[...]
        normed = knorm[hh]
        gg = un * kg_ref[...]
        out = krec[hh] * (gg - normed * jnp.mean(gg * normed, -1, keepdims=True))
        dk_ref[:, hh * D : (hh + 1) * D] = out.astype(BF16)
        dv_ref[:, hh * D : (hh + 1) * D] = acc[hh, 1].astype(BF16)

    total = collect(stages[2])
    qgg_ref[...] = total[0:1]
    kgg_ref[...] = total[1:2]
    for cp in given:
        cp.wait_send()

    kv_sends(lambda cp: cp.wait_send())
    for cp in kv_on_chip:
        cp.wait_send()
    auxc.wait_send()
    for cp in xc:
        cp.wait_send()

    def drain(slot, _):
        @pl.when(slot != own_slot)
        def _():
            for n in range(2):
                partial_copy(slot, n)[2].wait_send()

        return 0

    lax.fori_loop(0, slots, drain, 0)

    @pl.when(x == 1)
    def _():
        for m in range(2):
            for n in range(4):
                passing(m, n).wait_send()

    dq_near.wait()
    dq_far.wait_send()
    dq_far.wait_recv()


def emit(dq, dk, dv, qg, kg, dq_out, dk_out, dv_out, qg_out, kg_out, big, small, isem, osem):
    pieces = [(dk, small.at[0], dk_out), (dv, small.at[1], dv_out)]
    for n in range(4):
        rows = pl.ds(n * 64, 64)
        pieces.append((dq.at[rows], big.at[rows], dq_out.at[rows]))
    ins = [pltpu.make_async_copy(a, b, isem.at[n]) for n, (a, b, _) in enumerate(pieces)]
    outs = [pltpu.make_async_copy(b, o, osem.at[n]) for n, (_, b, o) in enumerate(pieces)]
    for cp in ins:
        cp.start()
    qg_out[...] = qg[0]
    kg_out[...] = kg[0]
    for a, b in zip(ins, outs):
        a.wait()
        b.start()
    for b in outs:
        b.wait()


def on_device(nz, q_raw, k_raw, values, saved_out, out_grad, q_gain, k_gain, ancestors):
    lanes = np.arange(D) % (D // 2)
    freq = jnp.asarray(
        np.exp(lanes * (-2.0 * math.log(ROPE_BASE) / D)).astype(np.float32)[None, :]
    )
    vm = pl.BlockSpec(memory_space=pltpu.VMEM)
    hbm = pl.BlockSpec(memory_space=pl.ANY)
    V = pltpu.VMEM
    dma = pltpu.SemaphoreType.DMA
    outs = pl.pallas_call(
        functools.partial(kernel, nz),
        out_shape=(
            jax.ShapeDtypeStruct(q_raw.shape, BF16),
            jax.ShapeDtypeStruct(k_raw.shape, BF16),
            jax.ShapeDtypeStruct(k_raw.shape, BF16),
            jax.ShapeDtypeStruct((1, D), F32),
            jax.ShapeDtypeStruct((1, D), F32),
        ),
        in_specs=[hbm, vm, vm, hbm, hbm, vm, vm, vm, vm],
        out_specs=(hbm, vm, vm, vm, vm),
        scratch_shapes=[
            V((2, T, HALF), BF16), V((2, T, HALF), BF16), V((2, T, HALF), BF16),
            V((9, 2, T, D), BF16), V((2, 2, T, D), BF16), V((9, D, T), BF16),
            V((2, 160, T), F32), V((T, D), F32), V((T, D), F32),
            V((2, T, D), F32), V((2, T, D), F32),
            V((2, D, G * T), BF16), V((2, G, D, T), F32), V((2, G, 1, T), F32),
            V((2, D, G * T), BF16), V((2, D, G * T), BF16), V((2, G, 1, T), F32), V((2, G, D, T), F32),
            V((2, G, 1, T), F32), V((13, T, G * T), BF16), V((13, T, G * T), BF16),
            V((T, T), F32), V((T, T), BF16), V((2, T, D), F32),
            V((9, 2, T, D), BF16), V((4, 2, T, D), BF16), V((5, 2, 2, T, D), BF16), V((2, T, HALF), BF16),
            V((D, T), F32), V((1, D), F32), V((2, BLK, D), F32), V((2, 32, D), F32),
            V((2, 2, T, D), F32),
            V((8, 8, D), F32), V((4, 8, D), F32), V((nz, 8, D), F32),
            dma((3,)), dma((4,)), dma((4,)), dma((2, 9)), dma((2, 9)),
            dma((2, 9)), dma((2, 5, 2)), dma((2, 4)), dma((2, 4)), dma, dma,
            dma((7,)), dma((8,)), dma((3,)), dma((4,)), dma((nz - 1,)), dma((nz,)),
        ],
        compiler_params=pltpu.CompilerParams(
            collective_id=0, has_side_effects=True, vmem_limit_bytes=63000000
        ),
    )(
        q_raw, k_raw, values, saved_out, out_grad,
        q_gain.reshape(1, D), k_gain.reshape(1, D), ancestors, freq,
    )
    return pl.pallas_call(
        emit,
        out_shape=(
            jax.ShapeDtypeStruct(q_raw.shape, BF16),
            jax.ShapeDtypeStruct(k_raw.shape, BF16),
            jax.ShapeDtypeStruct(k_raw.shape, BF16),
            jax.ShapeDtypeStruct((D,), F32),
            jax.ShapeDtypeStruct((D,), F32),
        ),
        in_specs=[hbm, hbm, hbm, vm, vm],
        out_specs=(hbm, hbm, hbm, vm, vm),
        scratch_shapes=[
            V(q_raw.shape, BF16), V((2,) + k_raw.shape, BF16), dma((6,)), dma((6,)),
        ],
    )(*outs)


def solution(mesh):
    nz = mesh.shape["ctx"] // 8
    wide = P("ctx", "heads")
    return jax.shard_map(
        functools.partial(on_device, nz),
        mesh=mesh,
        in_specs=(wide, wide, wide, wide, wide, P(), P(), P("ctx", None)),
        out_specs=(wide, wide, wide, P(), P()),
        check_vma=False,
    )
```
